512 devices in a mesh: gx: 32 (over y_lo, z), gy: 8 (over y_hi, x), depth: 2 (over core).
Axes of the slice: x: 4, y: 8 (y_hi: 2, y_lo: 4; y = y_hi * 4 + y_lo), z: 8, core: 2. Of those that a mesh axis runs over, the one named last changes fastest.
Arguments:
- adjoint: float32 [19, 24, 128, 4096], P(None, 'depth', 'gy', 'gx'), may hold values from -6 to 6
- momentum: float32 [3, 24, 128, 4096], P(None, 'depth', 'gy', 'gx'), may hold values from -4 to 4
- design: float32 [128, 4096], P('gy', 'gx'), may hold values from 0 to 1
- solid_mask: int32 [24, 128, 4096], P('depth', 'gy', 'gx'), may hold values 0 or 1
- port_label: int32 [24, 128, 4096], P('depth', 'gy', 'gx'), may hold values from 0 to 2, as said below
Outputs:
- new_adjoint: float32 [19, 24, 128, 4096], P(None, 'depth', 'gy', 'gx')
- sensitivity: float32 [128, 4096], P('gy', 'gx')
The draws below stay inside these ranges and needn't reach their ends.
Inputs may be any that keep to these rules, and one draw needn't show every extreme that they name: `solid_mask`: 1 marks a solid cell, 0 a fluid one. `port_label`: 0 marks an ordinary cell, 1 an inlet cell, 2 an outlet cell.
All inputs are finite; a program needn't handle non-finite values. No bound on the sum of `solid_mask` on one device may be relied on, other than what follows from the above.
Results may differ from the reference program's by a relative error of at most 0.00012.
Values sent between devices are 32-bit elements; how exact they have to be, the bound alone decides.
A program may use at most 128 MiB of HBM per device.

```python
import math
import jax
import jax.numpy as jnp
from jax import lax

VELOCITIES = 19
NX = 4096
NY = 128
NZ = 24


def draw_port_label(key, part):
    picks = jax.random.randint(key, (NZ, NY, NX), 0, 16)
    return jnp.where(picks == 0, 1, jnp.where(picks == 1, 2, 0)).astype(jnp.int32)


def set_ends(entries, own_key, low, top_value):
    shape = entries.shape
    place = [jax.random.randint(jax.random.fold_in(own_key, axis), (), 0, shape[axis]) for axis in range(len(shape))]
    entries = entries.at[tuple(place)].set(low)
    longest = shape.index(max(shape))
    place[longest] = (place[longest] + 1) % shape[longest]
    return entries.at[tuple(place)].set(top_value)


def block_scale(rng, dims, shards, low, top_value):
    gain = 1.0
    for dim, parts in shards:
        steps = jax.random.uniform(jax.random.fold_in(jax.random.fold_in(rng, 6), dim), (parts,), jnp.float32, low / len(shards), top_value / len(shards))
        gain = gain * jnp.repeat(jnp.exp(steps), dims[dim] // parts).reshape((-1,) + (1,) * (len(dims) - 1 - dim))
    return gain


def centred(key, shape, spread, reach, shards=(), dtype=jnp.bfloat16):
    array = jax.random.normal(key, shape, jnp.float32) * spread
    if len(shards) > 0:
        array = block_scale(key, shape, shards, -0.22, 0.18) * array
    return jnp.clip(array, min=-reach, max=reach).astype(dtype)


def setup_inputs(seed: int = 0) -> dict:
    arg_keys = jax.random.split(jax.random.key(seed), 6)
    adjoint = centred(arg_keys[0], (VELOCITIES, NZ, NY, NX), 1.0, 6.0, ((1, 2), (2, 8), (3, 32)), jnp.float32)
    momentum = centred(arg_keys[1], (3, NZ, NY, NX), 0.5, 4.0, ((1, 2), (2, 8), (3, 32)), jnp.float32)
    design = jnp.clip(1.0 * jax.random.uniform(arg_keys[2], (NY, NX), jnp.float32) ** block_scale(arg_keys[2], (NY, NX), ((0, 8), (1, 32)), -0.2, 0.2), 0.0, 1.0)
    solid_mask = set_ends((jax.random.randint(arg_keys[3], (NZ, NY, NX), 0, 8) < 1).astype(jnp.int32), jax.random.fold_in(arg_keys[3], 1), 0, 1)
    port_label = draw_port_label(jax.random.fold_in(arg_keys[5], 71), 0)
    return {"adjoint": adjoint, "momentum": momentum, "design": design, "solid_mask": solid_mask, "port_label": port_label}


velocities = ((0, 0, 0), (1, 0, 0), (-1, 0, 0), (0, 1, 0), (0, -1, 0), (0, 0, 1), (0, 0, -1), (1, 1, 0), (-1, -1, 0), (1, -1, 0), (-1, 1, 0), (1, 0, 1), (-1, 0, -1), (1, 0, -1), (-1, 0, 1), (0, 1, 1), (0, -1, -1), (0, 1, -1), (0, -1, 1))
lattice_weights = (1.0 / 3.0,) + (1.0 / 18.0,) * 6 + (1.0 / 36.0,) * 12
opposite = (0, 2, 1, 4, 3, 6, 5, 8, 7, 10, 9, 12, 11, 14, 13, 16, 15, 18, 17)
relax_rate = 1.25
damp_top = 0.5
cone_radius = 5.0
filter_reach = 4

def stream_pull(adjoint):
    depth_cells, band_cells, span_cells = adjoint.shape[1:]
    padded = jnp.pad(adjoint, ((0, 0), (1, 1), (1, 1), (1, 1)))
    pulled = []
    for number, vector in enumerate(velocities):
        pulled.append(padded[number, 1 + vector[2]:1 + vector[2] + depth_cells, 1 + vector[1]:1 + vector[1] + band_cells, 1 + vector[0]:1 + vector[0] + span_cells])
    return pulled

def collide(pulled, momentum, damping, solid_mask, port_label):
    zeroth = jnp.zeros_like(pulled[0])
    moment_x = jnp.zeros_like(pulled[0])
    moment_y = jnp.zeros_like(pulled[0])
    moment_z = jnp.zeros_like(pulled[0])
    for number, vector in enumerate(velocities):
        weighted = lattice_weights[number] * pulled[number]
        zeroth = zeroth + weighted
        if vector[0] != 0:
            moment_x = moment_x + vector[0] * weighted
        if vector[1] != 0:
            moment_y = moment_y + vector[1] * weighted
        if vector[2] != 0:
            moment_z = moment_z + vector[2] * weighted
    local_sens = -3.0 * (moment_x * momentum[0] + moment_y * momentum[1] + moment_z * momentum[2])
    fluid_cell = solid_mask == 0
    inlet_cell = port_label == 1
    outlet_cell = port_label == 2
    results = []
    for number, vector in enumerate(velocities):
        projected = 3.0 * (vector[0] * moment_x + vector[1] * moment_y + vector[2] * moment_z)
        relaxed = (1.0 - relax_rate) * pulled[number] + relax_rate * (zeroth + projected) - damping * projected
        updated = jnp.where(fluid_cell, relaxed, pulled[opposite[number]])
        updated = jnp.where(inlet_cell, 0.0, updated) + jnp.where(outlet_cell, float(vector[0]), 0.0)
        results.append(updated)
    kept_sens = jnp.where(fluid_cell & jnp.logical_not(inlet_cell), local_sens, 0.0)
    return (jnp.stack(results), kept_sens)

def cone_filter(column):
    band_cells, span_cells = column.shape
    padded = jnp.pad(column, filter_reach)
    ones_padded = jnp.pad(jnp.ones_like(column), filter_reach)
    numerator = jnp.zeros_like(column)
    denominator = jnp.zeros_like(column)
    for offset_y in range(-filter_reach, filter_reach + 1):
        for offset_x in range(-filter_reach, filter_reach + 1):
            weight = max(0.0, cone_radius - math.sqrt(offset_y * offset_y + offset_x * offset_x))
            if weight > 0.0:
                top = filter_reach + offset_y
                left = filter_reach + offset_x
                numerator = numerator + weight * padded[top:top + band_cells, left:left + span_cells]
                denominator = denominator + weight * ones_padded[top:top + band_cells, left:left + span_cells]
    return numerator / denominator

def reference(adjoint, momentum, design, solid_mask, port_label):
    damping = damp_top * (1.0 - design) / (1.0 + design)
    design_slope = -2.0 * damp_top / ((1.0 + design) * (1.0 + design))
    pulled = stream_pull(adjoint)
    new_adjoint, kept_sens = collide(pulled, momentum, damping, solid_mask, port_label)
    column = lax.optimization_barrier(jnp.sum(kept_sens, axis=0)) * design_slope
    return (new_adjoint, cone_filter(column))
```

```python
import functools
import math

import jax
import jax.numpy as jnp
from jax import lax
from jax.experimental import pallas as pl
from jax.experimental.pallas import tpu as pltpu
from jax.sharding import PartitionSpec as P

MESH = pl.DeviceIdType.MESH
F32 = jnp.float32
C = (
    (0, 0, 0),
    (1, 0, 0),
    (-1, 0, 0),
    (0, 1, 0),
    (0, -1, 0),
    (0, 0, 1),
    (0, 0, -1),
    (1, 1, 0),
    (-1, -1, 0),
    (1, -1, 0),
    (-1, 1, 0),
    (1, 0, 1),
    (-1, 0, -1),
    (1, 0, -1),
    (-1, 0, 1),
    (0, 1, 1),
    (0, -1, -1),
    (0, 1, -1),
    (0, -1, 1),
)
W = (1.0 / 3.0,) + (1.0 / 18.0,) * 6 + (1.0 / 36.0,) * 12
OPP = (0, 2, 1, 4, 3, 6, 5, 8, 7, 10, 9, 12, 11, 14, 13, 16, 15, 18, 17)
REACH = 4
PAD = 8
XR = (1, 7, 9, 11, 13)
XL = (2, 8, 10, 12, 14)
YU = (3, 7, 10, 15, 17)
YD = (4, 8, 9, 16, 18)
ZU = tuple(i for i in range(19) if C[i][2] == 1)
ZD = tuple(i for i in range(19) if C[i][2] == -1)
XS = XR + XL
BLK = 24


def cone(a, b):
    return max(0.0, 5.0 - math.sqrt(a * a + b * b))


def roll(v, shift, axis):
    size = v.shape[axis]
    if isinstance(shift, int):
        shift = shift % size
        if shift == 0:
            return v
    return pltpu.roll(v, shift, axis)


def lane_of(shape):
    return lax.broadcasted_iota(jnp.int32, shape, len(shape) - 1)


def row_of(shape):
    return lax.broadcasted_iota(jnp.int32, shape, len(shape) - 2)


def filtered(main, outer, tv):
    lane = lane_of((8, 128))
    sums = []
    for k in range(4):
        per_b = [main[k]]
        for b in range(1, REACH + 1):
            plus = jnp.where(lane < 128 - b, roll(main[k], -b, 1), roll(outer[k], -b, 1))
            minus = jnp.where(lane >= b, roll(main[k], b, 1), roll(outer[k], b, 1))
            per_b.append(plus + minus)
        sums.append(per_b)
    for a in range(REACH + 1):
        for k in range(4):
            total = None
            for b in range(REACH + 1):
                if cone(a, b) > 0.0:
                    term = cone(a, b) * sums[k][b]
                    total = term if total is None else total + term
            tv[a, 8 * k : 8 * k + 8, :] = total
    out = tv[0, 8:24, :]
    for a in range(1, REACH + 1):
        out = out + (tv[a, 8 - a : 24 - a, :] + tv[a, 8 + a : 24 + a, :])
    return out


def x_terms(pops, cm, cp):
    shape = (8, 128)
    lane, sub = lane_of(shape), row_of(shape)
    half = lane % 2
    block = lane // BLK
    ahead = roll(cp, -1, 0)
    ahead = jnp.where(sub < 7, ahead, jnp.where(half == 0, roll(ahead, -1, 1), 0.0))
    behind = roll(cp, 1, 0)
    behind = jnp.where(sub > 0, behind, jnp.where(half == 1, roll(behind, 1, 1), 0.0))
    src = cp
    for j in (1, 2):
        src = jnp.where(block == j, ahead if C[pops[j]][1] == 1 else behind, src)
    m0 = jnp.where(block == 0, cm, 0.0)
    m1 = jnp.where(block == 1, cm, 0.0)
    m2 = jnp.where(block == 2, cm, 0.0)
    u = m0
    for j in range(1, 5):
        u = u + roll(m0, BLK * j, 1)
    u = u * float(C[pops[0]][0])
    u = u + float(C[pops[1]][1]) * m1 + float(C[pops[2]][1]) * roll(m1, BLK, 1)
    u = u + float(C[pops[3]][2]) * roll(m2, BLK, 1) + float(C[pops[4]][2]) * roll(m2, 2 * BLK, 1)
    u = u * jnp.where(block == 0, 1.0 / 18.0, 1.0 / 36.0)
    prod = jnp.where(block < 5, u * src, 0.0)
    low = jnp.sum(jnp.where(half == 0, prod, 0.0), axis=1, keepdims=True)
    high = jnp.sum(jnp.where(half == 1, prod, 0.0), axis=1, keepdims=True)
    return low, high


def shift_ext(main, outer, cx):
    if cx == 0:
        return main, outer
    lane = lane_of(main.shape)
    a, b = roll(main, -cx, 1), roll(outer, -cx, 1)
    edge = lane == (127 if cx == 1 else 0)
    return jnp.where(edge, b, a), jnp.where(edge, a, b)


def kernel(
    adj, mom, des, sol, por,
    new, sens,
    adjv, momv, desv, solv, porv, mv, xs, yh, tv, den_v, ext,
    ym_s, ym_r, cp_s, cp_r, cm_s, cm_r, rl_s, rl_r, a0_s, a0_r, am_s, am_r, rm_s, rm_r, nu_s, nu_r,
    in_sem, pl_s, pl_r, ym_ss, ym_rs, cp_ss, cp_rs, cm_ss, cm_rs, rl_ss, rl_rs, a0_ss, a0_rs,
    am_ss, am_rs, rm_ss, rm_rs, nu_ss, nu_rs,
):
    gx, gy, core = lax.axis_index("gx"), lax.axis_index("gy"), lax.axis_index("depth")
    n_gx, n_gy = lax.axis_size("gx"), lax.axis_size("gy")
    has_x = (gx > 0, gx < n_gx - 1)
    has_y = (gy > 0, gy < n_gy - 1)
    to_x = ({"gx": gx - 1}, {"gx": gx + 1})
    to_y = ({"gy": gy - 1}, {"gy": gy + 1})
    to_p = {"depth": 1 - core}

    barrier = pltpu.get_barrier_semaphore()

    def tell(device):
        pl.semaphore_signal(barrier, inc=1, device_id=device, device_id_type=MESH)

    tell(to_p)
    for d in range(2):
        pl.when(has_x[d])(functools.partial(tell, to_x[d]))
        pl.when(has_y[d])(functools.partial(tell, to_y[d]))

    loads = [
        pltpu.make_async_copy(mom, momv, in_sem.at[19]),
        pltpu.make_async_copy(des, desv, in_sem.at[20]),
        pltpu.make_async_copy(sol, solv, in_sem.at[21]),
        pltpu.make_async_copy(por, porv, in_sem.at[22]),
    ]
    for i in range(19):
        start = PAD + (16 if C[i][2] == -1 else 0)
        loads.append(pltpu.make_async_copy(adj.at[i], adjv.at[i, pl.ds(start, 192), :], in_sem.at[i]))
    for copy in loads:
        copy.start()

    for d in range(2):

        def clear_x(d=d):
            for ref in (cp_r, cm_r, rl_r, a0_r):
                ref[d] = jnp.zeros_like(ref[d])

        def clear_y(d=d):
            for ref in (ym_r, am_r, rm_r):
                ref[d] = jnp.zeros_like(ref[d])

        pl.when(jnp.logical_not(has_x[d]))(clear_x)
        pl.when(jnp.logical_not(has_y[d]))(clear_y)

    @pl.when(core == 0)
    def _():
        for i in ZD:
            adjv[i, PAD : PAD + 16, :] = jnp.zeros((16, 128), F32)

    @pl.when(core == 1)
    def _():
        for i in ZU:
            adjv[i, PAD + 192 : PAD + 208, :] = jnp.zeros((16, 128), F32)

    peers = 1 + sum(here.astype(jnp.int32) for here in has_x + has_y)
    pl.semaphore_wait(barrier, peers)

    def planes(pops, src_row, dst_row):
        return [
            pltpu.make_async_remote_copy(
                src_ref=adj.at[i, pl.ds(src_row, 16), :],
                dst_ref=adjv.at[i, pl.ds(dst_row, 16), :],
                send_sem=pl_s.at[j],
                recv_sem=pl_r.at[j],
                device_id=to_p,
                device_id_type=MESH,
            )
            for j, i in enumerate(pops)
        ]

    plane_down = planes(ZD, 176, PAD)
    plane_up = planes(ZU, 0, PAD + 192)

    @pl.when(core == 0)
    def _():
        for copy in plane_down:
            copy.start()

    @pl.when(core == 1)
    def _():
        for copy in plane_up:
            copy.start()

    def remote(src, dst, s_sem, r_sem, d, device):
        return pltpu.make_async_remote_copy(
            src_ref=src.at[d],
            dst_ref=dst.at[1 - d],
            send_sem=s_sem.at[d],
            recv_sem=r_sem.at[1 - d],
            device_id=device,
            device_id_type=MESH,
        )

    def copies_x(d):
        return [
            remote(rl_s, rl_r, rl_ss, rl_rs, d, to_x[d]),
            remote(cp_s, cp_r, cp_ss, cp_rs, d, to_x[d]),
            remote(cm_s, cm_r, cm_ss, cm_rs, d, to_x[d]),
            remote(a0_s, a0_r, a0_ss, a0_rs, d, to_x[d]),
        ]

    cx = [copies_x(d) for d in range(2)]
    cym = [remote(ym_s, ym_r, ym_ss, ym_rs, d, to_y[d]) for d in range(2)]
    cam = [remote(am_s, am_r, am_ss, am_rs, d, to_y[d]) for d in range(2)]
    crm = [remote(rm_s, rm_r, rm_ss, rm_rs, d, to_y[d]) for d in range(2)]
    cnu = pltpu.make_async_remote_copy(
        src_ref=nu_s, dst_ref=nu_r, send_sem=nu_ss.at[0], recv_sem=nu_rs.at[0], device_id=to_p, device_id_type=MESH
    )

    for copy in loads[:4]:
        copy.wait()

    slope3 = 3.0 / ((1.0 + desv[...]) * (1.0 + desv[...]))

    @pl.loop(0, 12)
    def _(z):
        rows = pl.ds(pl.multiple_of(z * 16, 16), 16)
        keep = (solv[rows, :] == 0) & (porv[rows, :] != 1)
        scale = jnp.where(keep, slope3, 0.0)
        for k in range(3):
            mv[k, rows, :] = scale * momv[k, rows, :]

    for copy in loads[4:]:
        copy.wait()

    @pl.when(core == 0)
    def _():
        for copy in plane_up:
            copy.wait_recv()

    @pl.when(core == 1)
    def _():
        for copy in plane_down:
            copy.wait_recv()

    zo = [PAD + (16 if C[i][2] == 1 else 0) for i in range(19)]
    lane12 = lane_of((12, 128))
    lane8 = lane_of((8, 128))

    edge_rows = []
    for d, (pops, row) in enumerate(((YU, 0), (YD, 15))):
        values = [adjv[i, pl.ds(zo[i] + row, 12, stride=16), :] for i in pops]
        values += [mv[k, pl.ds(row, 12, stride=16), :] for k in range(3)]
        edge_rows.append(values)
        for v in range(8):
            ym_s[d, v] = values[v]
        pl.when(has_y[d])(cym[d].start)
    for d in range(2):
        packed = jnp.zeros((12, 128), F32)
        for l in range(2):
            for v in range(8):
                slot = 64 * l + 8 * v
                moved = roll(edge_rows[l][v], slot - (0 if d == 0 else 120), 1)
                packed = jnp.where((lane12 >= slot) & (lane12 < slot + 8), moved, packed)
        rl_s[d] = packed
        pl.when(has_x[d])(cx[d][0].start)

    def pack(z, carry):
        cp0, cp1, cm0, cm1 = carry
        for h in range(2):
            lane = 2 * z + h
            for j in range(5):
                at = lane + BLK * j
                row = pl.multiple_of(z * 16, 16) + 8 * h
                v0 = adjv[XR[j], pl.ds(zo[XR[j]] + row, 8), :]
                v1 = adjv[XL[j], pl.ds(zo[XL[j]] + row, 8), :]
                cp0 = jnp.where(lane8 == at, roll(v0, at, 1), cp0)
                cp1 = jnp.where(lane8 == at, roll(v1, at + 1, 1), cp1)
                if j < 3:
                    m = mv[j, pl.ds(row, 8), :]
                    cm0 = jnp.where(lane8 == at, roll(m, at, 1), cm0)
                    cm1 = jnp.where(lane8 == at, roll(m, at + 1, 1), cm1)
        return cp0, cp1, cm0, cm1

    zero8 = jnp.zeros((8, 128), F32)
    cp0, cp1, cm0, cm1 = lax.fori_loop(0, 12, pack, (zero8,) * 4)
    cp_s[0], cp_s[1], cm_s[0], cm_s[1] = cp0, cp1, cm0, cm1
    for d in range(2):
        pl.when(has_x[d])(cx[d][1].start)
        pl.when(has_x[d])(cx[d][2].start)

    lane16, row16 = lane_of((16, 128)), row_of((16, 128))

    def inner(z, total):
        base = pl.multiple_of(z * 16, 16)
        sums = [None, None, None]
        for i in range(1, 19):
            c = C[i]
            v = adjv[i, pl.ds(zo[i] + base + c[1], 16), :]
            if c[1] != 0:
                v = jnp.where(row16 == (15 if c[1] == 1 else 0), 0.0, v)
            if c[0] != 0:
                v = jnp.where(lane16 == (127 if c[0] == 1 else 0), 0.0, roll(v, -c[0], 1))
            v = W[i] * v
            for k in range(3):
                if c[k] != 0:
                    if sums[k] is None:
                        sums[k] = v * float(c[k])
                    else:
                        sums[k] = sums[k] + v if c[k] == 1 else sums[k] - v
        for k in range(3):
            total = total + sums[k] * mv[k, pl.ds(base, 16), :]
        return total

    a0 = lax.fori_loop(0, 12, inner, jnp.zeros((16, 128), F32))
    for d in range(2):
        a0_s[d] = a0
        pl.when(has_x[d])(cx[d][3].start)

    row8 = row_of((8, 128))
    ones, ones_out = [], []
    for k in range(4):
        y = gy * 16 + (row8 + (8 * k - 8))
        inside = (y >= 0) & (y < 16 * n_gy)
        ones.append(jnp.where(inside, 1.0, 0.0))
        x_out = jnp.where(lane8 < 64, gx * 128 + 128 + lane8, gx * 128 - 128 + lane8)
        ones_out.append(jnp.where(inside & (x_out >= 0) & (x_out < 128 * n_gx), 1.0, 0.0))
    den_v[...] = filtered(ones, ones_out, tv)

    for d in range(2):
        for copy in cx[1 - d]:
            pl.when(has_x[d])(copy.wait_recv)
    main = [a0[0:8], a0[8:16]]
    outer = [jnp.where(lane8 < 64, a0_r[1, 8 * h : 8 * h + 8, :], a0_r[0, 8 * h : 8 * h + 8, :]) for h in range(2)]
    own = (x_terms(XL, cm0, cp_r[0]), x_terms(XR, cm1, cp_r[1]))
    theirs = (x_terms(XR, cm_r[0], cp0), x_terms(XL, cm_r[1], cp1))
    for h in range(2):
        main[h] = main[h] + jnp.where(lane8 == 0, own[0][h], 0.0) + jnp.where(lane8 == 127, own[1][h], 0.0)
        outer[h] = outer[h] + jnp.where(lane8 == 127, theirs[0][h], 0.0) + jnp.where(lane8 == 0, theirs[1][h], 0.0)
    am_s[0] = jnp.where(row8 < 4, main[0], roll(outer[0], 4, 0))
    am_s[1] = jnp.where(row8 >= 4, main[1], roll(outer[1], 4, 0))
    left, right = rl_r[0], rl_r[1]
    rm_s[0] = jnp.where(lane12 < 64, right, roll(left, 64, 1))
    rm_s[1] = jnp.where(lane12 < 64, roll(right, 64, 1), left)
    for d in range(2):
        pl.when(has_y[d])(cam[d].start)
        pl.when(has_y[d])(crm[d].start)

    def move(z, carry):
        for h in range(2):
            row = pl.multiple_of(z * 16, 16) + 8 * h
            for n, i in enumerate(XS):
                at = 2 * z + h + BLK * (n % 5)
                v = adjv[i, pl.ds(zo[i] + row, 8), :]
                if n < 5:
                    v = jnp.where(lane8 == 127, roll(cp_r[1], 127 - at, 1), roll(v, -1, 1))
                else:
                    v = jnp.where(lane8 == 0, roll(cp_r[0], 128 - at, 1), roll(v, 1, 1))
                xs[n, pl.ds(PAD + row, 8), :] = v
        return carry

    lax.fori_loop(0, 12, move, 0)

    def ends(from_right, from_left, at_right, at_left):
        a = roll(from_right, -at_right, 1)
        b = roll(from_left, 120 - at_left, 1)
        return jnp.where(lane12 < 8, a, jnp.where(lane12 >= 120, b, 0.0))

    own_outer = [[ends(right, left, 64 * l + 8 * v, 64 * l + 8 * v) for v in range(8)] for l in range(2)]

    for d in range(2):
        pl.when(has_y[d])(cym[1 - d].wait_recv)
        pl.when(has_y[d])(cam[1 - d].wait_recv)
        pl.when(has_y[d])(crm[1 - d].wait_recv)

    def weighted(pops, moms, pulled):
        total = None
        for j, i in enumerate(pops):
            c = C[i]
            u = None
            for k in range(3):
                if c[k] != 0:
                    u = (moms[k] if c[k] == 1 else -moms[k]) if u is None else (u + moms[k] if c[k] == 1 else u - moms[k])
            term = (W[i] * u) * pulled[j]
            total = term if total is None else total + term
        return jnp.sum(total, axis=0, keepdims=True)

    inside_rows, beyond_rows = [], []
    for d, (mine, others) in enumerate(((YU, YD), (YD, YU))):
        got = [ym_r[d, v] for v in range(8)]
        got_outer = [ends(rm_r[d], rm_r[d], 8 * v, 64 + 8 * v) for v in range(8)]
        moved = [shift_ext(got[j], got_outer[j], C[others[j]][0]) for j in range(5)]
        for j in range(5):
            yh[d, j] = moved[j][0]
        inside_rows.append(
            (
                weighted(others, edge_rows[d][5:], [m[0] for m in moved]),
                weighted(others, own_outer[d][5:], [m[1] for m in moved]),
            )
        )
        moved = [shift_ext(edge_rows[d][j], own_outer[d][j], C[mine[j]][0]) for j in range(5)]
        beyond_rows.append(
            (weighted(mine, got[5:], [m[0] for m in moved]), weighted(mine, got_outer[5:], [m[1] for m in moved]))
        )

    top, bottom = am_r[0], am_r[1]
    blocks = [
        [jnp.where(row8 >= 4, top, 0.0), jnp.where(row8 >= 4, roll(top, 4, 0), 0.0)],
        [main[0], outer[0]],
        [main[1], outer[1]],
        [jnp.where(row8 < 4, bottom, 0.0), jnp.where(row8 < 4, roll(bottom, 4, 0), 0.0)],
    ]
    for part in range(2):
        blocks[0][part] = blocks[0][part] + jnp.where(row8 == 7, beyond_rows[0][part], 0.0)
        blocks[1][part] = blocks[1][part] + jnp.where(row8 == 0, inside_rows[0][part], 0.0)
        blocks[2][part] = blocks[2][part] + jnp.where(row8 == 7, inside_rows[1][part], 0.0)
        blocks[3][part] = blocks[3][part] + jnp.where(row8 == 0, beyond_rows[1][part], 0.0)
    number = filtered([b[0] for b in blocks], [b[1] for b in blocks], tv)
    nu_s[...] = number
    cnu.start()

    damping = 0.5 * (1.0 - desv[...]) / (1.0 + desv[...])

    @pl.loop(0, 12)
    def _(z):
        base = pl.multiple_of(z * 16, 16)
        rows = pl.ds(base, 16)
        pulled = []
        for i in range(19):
            c = C[i]
            if c[0] != 0:
                v = xs[XS.index(i), pl.ds(PAD + base + c[1], 16), :]
            else:
                v = adjv[i, pl.ds(zo[i] + base + c[1], 16), :]
            if c[1] == 1:
                v = jnp.where(row16 == 15, yh[1, YU.index(i), pl.ds(z, 1), :], v)
            elif c[1] == -1:
                v = jnp.where(row16 == 0, yh[0, YD.index(i), pl.ds(z, 1), :], v)
            pulled.append(v)
        zeroth = W[0] * pulled[0]
        sums = [jnp.zeros((16, 128), F32)] * 3
        for i in range(1, 19):
            v = W[i] * pulled[i]
            zeroth = zeroth + v
            for k in range(3):
                if C[i][k] == 1:
                    sums[k] = sums[k] + v
                elif C[i][k] == -1:
                    sums[k] = sums[k] - v
        gain = (1.25 - damping) * 3.0
        sums = [gain * s for s in sums]
        base_term = 1.25 * zeroth
        fluid = solv[rows, :] == 0
        port = porv[rows, :]
        inlet, outlet = port == 1, port == 2
        bump = jnp.where(outlet, 1.0, 0.0)
        for i in range(19):
            c = C[i]
            relaxed = base_term - 0.25 * pulled[i]
            for k in range(3):
                if c[k] == 1:
                    relaxed = relaxed + sums[k]
                elif c[k] == -1:
                    relaxed = relaxed - sums[k]
            out = jnp.where(fluid, relaxed, pulled[OPP[i]])
            out = jnp.where(inlet, 0.0, out)
            if c[0] == 1:
                out = out + bump
            elif c[0] == -1:
                out = out - bump
            new[i, rows, :] = out

    cnu.wait_recv()
    sens[...] = (number + nu_r[...]) / den_v[...]

    @pl.when(core == 0)
    def _():
        for copy in plane_down:
            copy.wait_send()

    @pl.when(core == 1)
    def _():
        for copy in plane_up:
            copy.wait_send()

    for d in range(2):
        for copy in cx[d]:
            pl.when(has_x[d])(copy.wait_send)
        for copy in (cym[d], cam[d], crm[d]):
            pl.when(has_y[d])(copy.wait_send)
    cnu.wait_send()


def on_device(adjoint, momentum, design, solid_mask, port_label):
    hbm = pl.BlockSpec(memory_space=pl.ANY)
    vmem = pl.BlockSpec(memory_space=pltpu.VMEM)
    dma = pltpu.SemaphoreType.DMA
    v = lambda *shape, t=F32: pltpu.VMEM(shape, t)
    buffers = [
        v(19, 224, 128), v(3, 192, 128), v(16, 128), v(192, 128, t=jnp.int32), v(192, 128, t=jnp.int32),
        v(3, 192, 128), v(10, 208, 128), v(2, 5, 12, 128), v(5, 32, 128), v(16, 128), v(8, 128),
    ]
    messages = [(8, 12, 128), (8, 128), (8, 128), (12, 128), (16, 128), (8, 128), (12, 128)]
    for shape in messages:
        buffers += [v(2, *shape), v(2, *shape)]
    buffers += [v(16, 128), v(16, 128)]
    sems = [dma((23,)), dma((5,)), dma((5,))] + [dma((2,))] * 14 + [dma((1,))] * 2
    new, sens = pl.pallas_call(
        kernel,
        out_shape=(jax.ShapeDtypeStruct((19, 192, 128), F32), jax.ShapeDtypeStruct((16, 128), F32)),
        in_specs=[hbm] * 5,
        out_specs=(vmem, vmem),
        scratch_shapes=buffers + sems,
        compiler_params=pltpu.CompilerParams(collective_id=0, has_side_effects=True),
    )(
        adjoint.reshape(19, 192, 128),
        momentum.reshape(3, 192, 128),
        design,
        solid_mask.reshape(192, 128),
        port_label.reshape(192, 128),
    )
    return new.reshape(19, 12, 16, 128), sens


def solution(mesh):
    cells = P("depth", "gy", "gx")
    fields = P(None, "depth", "gy", "gx")
    plane = P("gy", "gx")
    return jax.shard_map(
        on_device,
        mesh=mesh,
        in_specs=(fields, fields, plane, cells, cells),
        out_specs=(fields, plane),
        check_vma=False,
    )
```

```python
import functools
import math

import jax
import jax.numpy as jnp
from jax import lax
from jax.experimental import pallas as pl
from jax.experimental.pallas import tpu as pltpu
from jax.sharding import PartitionSpec as P

MESH = pl.DeviceIdType.MESH
F32 = jnp.float32
C = (
    (0, 0, 0),
    (1, 0, 0),
    (-1, 0, 0),
    (0, 1, 0),
    (0, -1, 0),
    (0, 0, 1),
    (0, 0, -1),
    (1, 1, 0),
    (-1, -1, 0),
    (1, -1, 0),
    (-1, 1, 0),
    (1, 0, 1),
    (-1, 0, -1),
    (1, 0, -1),
    (-1, 0, 1),
    (0, 1, 1),
    (0, -1, -1),
    (0, 1, -1),
    (0, -1, 1),
)
W = (1.0 / 3.0,) + (1.0 / 18.0,) * 6 + (1.0 / 36.0,) * 12
OPP = (0, 2, 1, 4, 3, 6, 5, 8, 7, 10, 9, 12, 11, 14, 13, 16, 15, 18, 17)
REACH = 4
PAD = 8
XR = (1, 7, 9, 11, 13)
XL = (2, 8, 10, 12, 14)
YU = (3, 7, 10, 15, 17)
YD = (4, 8, 9, 16, 18)
ZU = tuple(i for i in range(19) if C[i][2] == 1)
ZD = tuple(i for i in range(19) if C[i][2] == -1)
XS = XR + XL
BLK = 24


def cone(a, b):
    return max(0.0, 5.0 - math.sqrt(a * a + b * b))


def roll(v, shift, axis):
    size = v.shape[axis]
    if isinstance(shift, int):
        shift = shift % size
        if shift == 0:
            return v
    return pltpu.roll(v, shift, axis)


def lane_of(shape):
    return lax.broadcasted_iota(jnp.int32, shape, len(shape) - 1)


def row_of(shape):
    return lax.broadcasted_iota(jnp.int32, shape, len(shape) - 2)


def filtered(main, outer, tv):
    lane = lane_of((8, 128))
    sums = []
    for k in range(4):
        per_b = [main[k]]
        for b in range(1, REACH + 1):
            plus = jnp.where(lane < 128 - b, roll(main[k], -b, 1), roll(outer[k], -b, 1))
            minus = jnp.where(lane >= b, roll(main[k], b, 1), roll(outer[k], b, 1))
            per_b.append(plus + minus)
        sums.append(per_b)
    for a in range(REACH + 1):
        for k in range(4):
            total = None
            for b in range(REACH + 1):
                if cone(a, b) > 0.0:
                    term = cone(a, b) * sums[k][b]
                    total = term if total is None else total + term
            tv[a, 8 * k : 8 * k + 8, :] = total
    out = tv[0, 8:24, :]
    for a in range(1, REACH + 1):
        out = out + (tv[a, 8 - a : 24 - a, :] + tv[a, 8 + a : 24 + a, :])
    return out


def x_terms(pops, cm, cp):
    shape = (8, 128)
    lane, sub = lane_of(shape), row_of(shape)
    half = lane % 2
    block = lane // BLK
    ahead = roll(cp, -1, 0)
    ahead = jnp.where(sub < 7, ahead, jnp.where(half == 0, roll(ahead, -1, 1), 0.0))
    behind = roll(cp, 1, 0)
    behind = jnp.where(sub > 0, behind, jnp.where(half == 1, roll(behind, 1, 1), 0.0))
    src = cp
    for j in (1, 2):
        src = jnp.where(block == j, ahead if C[pops[j]][1] == 1 else behind, src)
    m0 = jnp.where(block == 0, cm, 0.0)
    m1 = jnp.where(block == 1, cm, 0.0)
    m2 = jnp.where(block == 2, cm, 0.0)
    u = m0
    for j in range(1, 5):
        u = u + roll(m0, BLK * j, 1)
    u = u * float(C[pops[0]][0])
    u = u + float(C[pops[1]][1]) * m1 + float(C[pops[2]][1]) * roll(m1, BLK, 1)
    u = u + float(C[pops[3]][2]) * roll(m2, BLK, 1) + float(C[pops[4]][2]) * roll(m2, 2 * BLK, 1)
    u = u * jnp.where(block == 0, 1.0 / 18.0, 1.0 / 36.0)
    prod = jnp.where(block < 5, u * src, 0.0)
    low = jnp.sum(jnp.where(half == 0, prod, 0.0), axis=1, keepdims=True)
    high = jnp.sum(jnp.where(half == 1, prod, 0.0), axis=1, keepdims=True)
    return low, high


def shift_ext(main, outer, cx):
    if cx == 0:
        return main, outer
    lane = lane_of(main.shape)
    a, b = roll(main, -cx, 1), roll(outer, -cx, 1)
    edge = lane == (127 if cx == 1 else 0)
    return jnp.where(edge, b, a), jnp.where(edge, a, b)


def kernel(
    adj, mom, des, sol, por,
    new, sens,
    adjv, halo, momv, desv, solv, porv, mv, xs, yh, tv, den_v, ext,
    ym_s, ym_r, cp_s, cp_r, cm_s, cm_r, rl_s, rl_r, a0_s, a0_r, am_s, am_r, rm_s, rm_r, nu_s, nu_r,
    in_sem, pl_s, pl_r, ym_ss, ym_rs, cp_ss, cp_rs, cm_ss, cm_rs, rl_ss, rl_rs, a0_ss, a0_rs,
    am_ss, am_rs, rm_ss, rm_rs, nu_ss, nu_rs, x_in, y_in,
):
    gx, gy, core = lax.axis_index("gx"), lax.axis_index("gy"), lax.axis_index("depth")
    n_gx, n_gy = lax.axis_size("gx"), lax.axis_size("gy")
    has_x = (gx > 0, gx < n_gx - 1)
    has_y = (gy > 0, gy < n_gy - 1)
    to_x = ({"gx": gx - 1}, {"gx": gx + 1})
    to_y = ({"gy": gy - 1}, {"gy": gy + 1})
    to_p = {"depth": 1 - core}

    barrier = pltpu.get_barrier_semaphore()

    def tell(device):
        pl.semaphore_signal(barrier, inc=1, device_id=device, device_id_type=MESH)

    tell(to_p)
    for d in range(2):
        pl.when(has_x[d])(functools.partial(tell, {**to_x[d], "depth": 0}))
        pl.when(has_y[d])(functools.partial(tell, {**to_y[d], "depth": 1}))

    def know(counter, other_sem, has):
        @pl.when(core == counter)
        def _():
            pl.semaphore_wait(barrier, 1 + 2 * sum(here.astype(jnp.int32) for here in has))
            pl.semaphore_signal(other_sem, inc=1, device_id=to_p, device_id_type=MESH)

        @pl.when(core != counter)
        def _():
            pl.semaphore_wait(other_sem, 1)

    know_x = functools.partial(know, 0, x_in, has_x)
    know_y = functools.partial(know, 1, y_in, has_y)
    y_first = gx % 8 < 4
    x_first = jnp.logical_not(y_first)

    loads = [
        pltpu.make_async_copy(mom, momv, in_sem.at[19]),
        pltpu.make_async_copy(des, desv, in_sem.at[20]),
        pltpu.make_async_copy(sol, solv, in_sem.at[21]),
        pltpu.make_async_copy(por, porv, in_sem.at[22]),
    ]
    for i in range(19):
        start = PAD + (16 if C[i][2] == -1 else 0)
        loads.append(pltpu.make_async_copy(adj.at[i], adjv.at[i, pl.ds(start, 192), :], in_sem.at[i]))
    for copy in loads:
        copy.start()

    for d in range(2):

        def clear_x(d=d):
            for ref in (cp_r, cm_r, rl_r, a0_r):
                ref[d] = jnp.zeros_like(ref[d])

        def clear_y(d=d):
            for ref in (ym_r, am_r, rm_r):
                ref[d] = jnp.zeros_like(ref[d])

        pl.when(jnp.logical_not(has_x[d]))(clear_x)
        pl.when(jnp.logical_not(has_y[d]))(clear_y)

    @pl.when(core == 0)
    def _():
        for i in ZD:
            adjv[i, PAD : PAD + 16, :] = jnp.zeros((16, 128), F32)

    @pl.when(core == 1)
    def _():
        for i in ZU:
            adjv[i, PAD + 192 : PAD + 208, :] = jnp.zeros((16, 128), F32)

    def planes(pops, src_row):
        return [
            pltpu.make_async_remote_copy(
                src_ref=adj.at[i, pl.ds(src_row, 16), :],
                dst_ref=halo.at[j],
                send_sem=pl_s.at[j],
                recv_sem=pl_r.at[j],
                device_id=to_p,
                device_id_type=MESH,
            )
            for j, i in enumerate(pops)
        ]

    plane_down = planes(ZD, 176)
    plane_up = planes(ZU, 0)

    def send_planes():
        @pl.when(core == 0)
        def _():
            for copy in plane_down:
                copy.start()

        @pl.when(core == 1)
        def _():
            for copy in plane_up:
                copy.start()

    @pl.when(x_first)
    def _():
        know_x()
        send_planes()

    def remote(src, dst, s_sem, r_sem, d, device):
        return pltpu.make_async_remote_copy(
            src_ref=src.at[d],
            dst_ref=dst.at[1 - d],
            send_sem=s_sem.at[d],
            recv_sem=r_sem.at[1 - d],
            device_id=device,
            device_id_type=MESH,
        )

    def copies_x(d):
        return [
            remote(rl_s, rl_r, rl_ss, rl_rs, d, to_x[d]),
            remote(cp_s, cp_r, cp_ss, cp_rs, d, to_x[d]),
            remote(cm_s, cm_r, cm_ss, cm_rs, d, to_x[d]),
            remote(a0_s, a0_r, a0_ss, a0_rs, d, to_x[d]),
        ]

    cx = [copies_x(d) for d in range(2)]
    cym = [remote(ym_s, ym_r, ym_ss, ym_rs, d, to_y[d]) for d in range(2)]
    cam = [remote(am_s, am_r, am_ss, am_rs, d, to_y[d]) for d in range(2)]
    crm = [remote(rm_s, rm_r, rm_ss, rm_rs, d, to_y[d]) for d in range(2)]
    cnu = pltpu.make_async_remote_copy(
        src_ref=nu_s, dst_ref=nu_r, send_sem=nu_ss.at[0], recv_sem=nu_rs.at[0], device_id=to_p, device_id_type=MESH
    )

    for copy in loads[:4]:
        copy.wait()

    slope3 = 3.0 / ((1.0 + desv[...]) * (1.0 + desv[...]))

    @pl.loop(0, 12)
    def _(z):
        rows = pl.ds(pl.multiple_of(z * 16, 16), 16)
        keep = (solv[rows, :] == 0) & (porv[rows, :] != 1)
        scale = jnp.where(keep, slope3, 0.0)
        for k in range(3):
            mv[k, rows, :] = scale * momv[k, rows, :]

    for copy in loads[4:]:
        copy.wait()

    zo = [PAD + (16 if C[i][2] == 1 else 0) for i in range(19)]
    lane12 = lane_of((12, 128))
    lane8 = lane_of((8, 128))

    def pack(z, carry):
        cp0, cp1, cm0, cm1 = carry
        for h in range(2):
            lane = 2 * z + h
            for j in range(5):
                at = lane + BLK * j
                row = pl.multiple_of(z * 16, 16) + 8 * h
                v0 = adjv[XR[j], pl.ds(zo[XR[j]] + row, 8), :]
                v1 = adjv[XL[j], pl.ds(zo[XL[j]] + row, 8), :]
                cp0 = jnp.where(lane8 == at, roll(v0, at, 1), cp0)
                cp1 = jnp.where(lane8 == at, roll(v1, at + 1, 1), cp1)
                if j < 3:
                    m = mv[j, pl.ds(row, 8), :]
                    cm0 = jnp.where(lane8 == at, roll(m, at, 1), cm0)
                    cm1 = jnp.where(lane8 == at, roll(m, at + 1, 1), cm1)
        return cp0, cp1, cm0, cm1

    lane16, row16 = lane_of((16, 128)), row_of((16, 128))

    def inner(z, total):
        base = pl.multiple_of(z * 16, 16)
        sums = [None, None, None]
        for i in range(1, 19):
            c = C[i]
            v = adjv[i, pl.ds(zo[i] + base + c[1], 16), :]
            if c[1] != 0:
                v = jnp.where(row16 == (15 if c[1] == 1 else 0), 0.0, v)
            if c[0] != 0:
                v = jnp.where(lane16 == (127 if c[0] == 1 else 0), 0.0, roll(v, -c[0], 1))
            v = W[i] * v
            for k in range(3):
                if c[k] != 0:
                    if sums[k] is None:
                        sums[k] = v * float(c[k])
                    else:
                        sums[k] = sums[k] + v if c[k] == 1 else sums[k] - v
        for k in range(3):
            total = total + sums[k] * mv[k, pl.ds(base, 16), :]
        return total


    def both(z, carry):
        return (*pack(z, carry[:4]), inner(z, carry[4]))

    zero8 = jnp.zeros((8, 128), F32)
    start = (zero8, zero8, zero8, zero8, jnp.zeros((16, 128), F32))
    carry = lax.fori_loop(core, core + 11, both, start)

    @pl.when(y_first)
    def _():
        know_y()
        send_planes()

    @pl.when(core == 0)
    def _():
        for copy in plane_up:
            copy.wait_recv()
        for j, i in enumerate(ZU):
            adjv[i, PAD + 192 : PAD + 208, :] = halo[j]

    @pl.when(core == 1)
    def _():
        for copy in plane_down:
            copy.wait_recv()
        for j, i in enumerate(ZD):
            adjv[i, PAD : PAD + 16, :] = halo[j]

    cp0, cp1, cm0, cm1, a0 = both(11 * (1 - core), carry)
    cp_s[0], cp_s[1], cm_s[0], cm_s[1] = cp0, cp1, cm0, cm1

    edge_rows = []
    for d, (pops, row) in enumerate(((YU, 0), (YD, 15))):
        values = [adjv[i, pl.ds(zo[i] + row, 12, stride=16), :] for i in pops]
        values += [mv[k, pl.ds(row, 12, stride=16), :] for k in range(3)]
        edge_rows.append(values)
        for v in range(8):
            ym_s[d, v] = values[v]
    for d in range(2):
        packed = jnp.zeros((12, 128), F32)
        for l in range(2):
            for v in range(8):
                slot = 64 * l + 8 * v
                moved = roll(edge_rows[l][v], slot - (0 if d == 0 else 120), 1)
                packed = jnp.where((lane12 >= slot) & (lane12 < slot + 8), moved, packed)
        rl_s[d] = packed
        a0_s[d] = a0

    def send_y():
        for d in range(2):
            pl.when(has_y[d])(cym[d].start)

    @pl.when(y_first)
    def _():
        send_y()
        know_x()

    for d in range(2):
        for copy in cx[d]:
            pl.when(has_x[d])(copy.start)

    @pl.when(x_first)
    def _():
        know_y()
        send_y()

    row8 = row_of((8, 128))
    ones, ones_out = [], []
    for k in range(4):
        y = gy * 16 + (row8 + (8 * k - 8))
        inside = (y >= 0) & (y < 16 * n_gy)
        ones.append(jnp.where(inside, 1.0, 0.0))
        x_out = jnp.where(lane8 < 64, gx * 128 + 128 + lane8, gx * 128 - 128 + lane8)
        ones_out.append(jnp.where(inside & (x_out >= 0) & (x_out < 128 * n_gx), 1.0, 0.0))
    den_v[...] = filtered(ones, ones_out, tv)

    for d in range(2):
        for copy in cx[1 - d]:
            pl.when(has_x[d])(copy.wait_recv)
    main = [a0[0:8], a0[8:16]]
    outer = [jnp.where(lane8 < 64, a0_r[1, 8 * h : 8 * h + 8, :], a0_r[0, 8 * h : 8 * h + 8, :]) for h in range(2)]
    own = (x_terms(XL, cm0, cp_r[0]), x_terms(XR, cm1, cp_r[1]))
    theirs = (x_terms(XR, cm_r[0], cp0), x_terms(XL, cm_r[1], cp1))
    for h in range(2):
        main[h] = main[h] + jnp.where(lane8 == 0, own[0][h], 0.0) + jnp.where(lane8 == 127, own[1][h], 0.0)
        outer[h] = outer[h] + jnp.where(lane8 == 127, theirs[0][h], 0.0) + jnp.where(lane8 == 0, theirs[1][h], 0.0)
    am_s[0] = jnp.where(row8 < 4, main[0], roll(outer[0], 4, 0))
    am_s[1] = jnp.where(row8 >= 4, main[1], roll(outer[1], 4, 0))
    left, right = rl_r[0], rl_r[1]
    rm_s[0] = jnp.where(lane12 < 64, right, roll(left, 64, 1))
    rm_s[1] = jnp.where(lane12 < 64, roll(right, 64, 1), left)
    for d in range(2):
        pl.when(has_y[d])(cam[d].start)
        pl.when(has_y[d])(crm[d].start)

    def move(z, carry):
        for h in range(2):
            row = pl.multiple_of(z * 16, 16) + 8 * h
            for n, i in enumerate(XS):
                at = 2 * z + h + BLK * (n % 5)
                v = adjv[i, pl.ds(zo[i] + row, 8), :]
                if n < 5:
                    v = jnp.where(lane8 == 127, roll(cp_r[1], 127 - at, 1), roll(v, -1, 1))
                else:
                    v = jnp.where(lane8 == 0, roll(cp_r[0], 128 - at, 1), roll(v, 1, 1))
                xs[n, pl.ds(PAD + row, 8), :] = v
        return carry

    lax.fori_loop(0, 12, move, 0)

    def ends(from_right, from_left, at_right, at_left):
        a = roll(from_right, -at_right, 1)
        b = roll(from_left, 120 - at_left, 1)
        return jnp.where(lane12 < 8, a, jnp.where(lane12 >= 120, b, 0.0))

    own_outer = [[ends(right, left, 64 * l + 8 * v, 64 * l + 8 * v) for v in range(8)] for l in range(2)]

    for d in range(2):
        pl.when(has_y[d])(cym[1 - d].wait_recv)
        pl.when(has_y[d])(cam[1 - d].wait_recv)
        pl.when(has_y[d])(crm[1 - d].wait_recv)

    def weighted(pops, moms, pulled):
        total = None
        for j, i in enumerate(pops):
            c = C[i]
            u = None
            for k in range(3):
                if c[k] != 0:
                    u = (moms[k] if c[k] == 1 else -moms[k]) if u is None else (u + moms[k] if c[k] == 1 else u - moms[k])
            term = (W[i] * u) * pulled[j]
            total = term if total is None else total + term
        return jnp.sum(total, axis=0, keepdims=True)

    inside_rows, beyond_rows = [], []
    for d, (mine, others) in enumerate(((YU, YD), (YD, YU))):
        got = [ym_r[d, v] for v in range(8)]
        got_outer = [ends(rm_r[d], rm_r[d], 8 * v, 64 + 8 * v) for v in range(8)]
        moved = [shift_ext(got[j], got_outer[j], C[others[j]][0]) for j in range(5)]
        for j in range(5):
            yh[d, j] = moved[j][0]
        inside_rows.append(
            (
                weighted(others, edge_rows[d][5:], [m[0] for m in moved]),
                weighted(others, own_outer[d][5:], [m[1] for m in moved]),
            )
        )
        moved = [shift_ext(edge_rows[d][j], own_outer[d][j], C[mine[j]][0]) for j in range(5)]
        beyond_rows.append(
            (weighted(mine, got[5:], [m[0] for m in moved]), weighted(mine, got_outer[5:], [m[1] for m in moved]))
        )

    top, bottom = am_r[0], am_r[1]
    blocks = [
        [jnp.where(row8 >= 4, top, 0.0), jnp.where(row8 >= 4, roll(top, 4, 0), 0.0)],
        [main[0], outer[0]],
        [main[1], outer[1]],
        [jnp.where(row8 < 4, bottom, 0.0), jnp.where(row8 < 4, roll(bottom, 4, 0), 0.0)],
    ]
    for part in range(2):
        blocks[0][part] = blocks[0][part] + jnp.where(row8 == 7, beyond_rows[0][part], 0.0)
        blocks[1][part] = blocks[1][part] + jnp.where(row8 == 0, inside_rows[0][part], 0.0)
        blocks[2][part] = blocks[2][part] + jnp.where(row8 == 7, inside_rows[1][part], 0.0)
        blocks[3][part] = blocks[3][part] + jnp.where(row8 == 0, beyond_rows[1][part], 0.0)
    number = filtered([b[0] for b in blocks], [b[1] for b in blocks], tv)
    nu_s[...] = number
    cnu.start()

    damping = 0.5 * (1.0 - desv[...]) / (1.0 + desv[...])

    @pl.loop(0, 12)
    def _(z):
        base = pl.multiple_of(z * 16, 16)
        rows = pl.ds(base, 16)
        pulled = []
        for i in range(19):
            c = C[i]
            if c[0] != 0:
                v = xs[XS.index(i), pl.ds(PAD + base + c[1], 16), :]
            else:
                v = adjv[i, pl.ds(zo[i] + base + c[1], 16), :]
            if c[1] == 1:
                v = jnp.where(row16 == 15, yh[1, YU.index(i), pl.ds(z, 1), :], v)
            elif c[1] == -1:
                v = jnp.where(row16 == 0, yh[0, YD.index(i), pl.ds(z, 1), :], v)
            pulled.append(v)
        zeroth = W[0] * pulled[0]
        sums = [jnp.zeros((16, 128), F32)] * 3
        for i in range(1, 19):
            v = W[i] * pulled[i]
            zeroth = zeroth + v
            for k in range(3):
                if C[i][k] == 1:
                    sums[k] = sums[k] + v
                elif C[i][k] == -1:
                    sums[k] = sums[k] - v
        gain = (1.25 - damping) * 3.0
        sums = [gain * s for s in sums]
        base_term = 1.25 * zeroth
        fluid = solv[rows, :] == 0
        port = porv[rows, :]
        inlet, outlet = port == 1, port == 2
        bump = jnp.where(outlet, 1.0, 0.0)
        for i in range(19):
            c = C[i]
            relaxed = base_term - 0.25 * pulled[i]
            for k in range(3):
                if c[k] == 1:
                    relaxed = relaxed + sums[k]
                elif c[k] == -1:
                    relaxed = relaxed - sums[k]
            out = jnp.where(fluid, relaxed, pulled[OPP[i]])
            out = jnp.where(inlet, 0.0, out)
            if c[0] == 1:
                out = out + bump
            elif c[0] == -1:
                out = out - bump
            new[i, rows, :] = out

    cnu.wait_recv()
    sens[...] = (number + nu_r[...]) / den_v[...]

    @pl.when(core == 0)
    def _():
        for copy in plane_down:
            copy.wait_send()

    @pl.when(core == 1)
    def _():
        for copy in plane_up:
            copy.wait_send()

    for d in range(2):
        for copy in cx[d]:
            pl.when(has_x[d])(copy.wait_send)
        for copy in (cym[d], cam[d], crm[d]):
            pl.when(has_y[d])(copy.wait_send)
    cnu.wait_send()


def write_out(new_v, sens_v, new, sens, sem):
    copies = [pltpu.make_async_copy(new_v.at[i], new.at[i], sem.at[i]) for i in range(19)]
    copies.append(pltpu.make_async_copy(sens_v, sens, sem.at[19]))
    for copy in copies:
        copy.start()
    for copy in copies:
        copy.wait()


def on_device(adjoint, momentum, design, solid_mask, port_label):
    hbm = pl.BlockSpec(memory_space=pl.ANY)
    vmem = pl.BlockSpec(memory_space=pltpu.VMEM)
    dma = pltpu.SemaphoreType.DMA
    v = lambda *shape, t=F32: pltpu.VMEM(shape, t)
    buffers = [
        v(19, 224, 128), v(5, 16, 128), v(3, 192, 128), v(16, 128), v(192, 128, t=jnp.int32), v(192, 128, t=jnp.int32),
        v(3, 192, 128), v(10, 208, 128), v(2, 5, 12, 128), v(5, 32, 128), v(16, 128), v(8, 128),
    ]
    messages = [(8, 12, 128), (8, 128), (8, 128), (12, 128), (16, 128), (8, 128), (12, 128)]
    for shape in messages:
        buffers += [v(2, *shape), v(2, *shape)]
    buffers += [v(16, 128), v(16, 128)]
    sems = [dma((23,)), dma((5,)), dma((5,))] + [dma((2,))] * 14 + [dma((1,))] * 2 + [pltpu.SemaphoreType.REGULAR] * 2
    new, sens = pl.pallas_call(
        kernel,
        out_shape=(v(19, 192, 128), v(16, 128)),
        in_specs=[hbm] * 5,
        out_specs=(vmem, vmem),
        scratch_shapes=buffers + sems,
        compiler_params=pltpu.CompilerParams(collective_id=0, has_side_effects=True),
    )(
        adjoint.reshape(19, 192, 128),
        momentum.reshape(3, 192, 128),
        design,
        solid_mask.reshape(192, 128),
        port_label.reshape(192, 128),
    )
    new, sens = pl.pallas_call(
        write_out,
        out_shape=(jax.ShapeDtypeStruct((19, 192, 128), F32), jax.ShapeDtypeStruct((16, 128), F32)),
        in_specs=[vmem, vmem],
        out_specs=(hbm, hbm),
        scratch_shapes=[dma((20,))],
    )(*(pltpu.with_memory_space_constraint(x, pltpu.VMEM) for x in (new, sens)))
    return new.reshape(19, 12, 16, 128), sens


def solution(mesh):
    cells = P("depth", "gy", "gx")
    fields = P(None, "depth", "gy", "gx")
    plane = P("gy", "gx")
    return jax.shard_map(
        on_device,
        mesh=mesh,
        in_specs=(fields, fields, plane, cells, cells),
        out_specs=(fields, plane),
        check_vma=False,
    )
```

```python
import functools
import math

import jax
import jax.numpy as jnp
from jax import lax
from jax.experimental import pallas as pl
from jax.experimental.pallas import tpu as pltpu
from jax.sharding import PartitionSpec as P

MESH = pl.DeviceIdType.MESH
F32 = jnp.float32
C = (
    (0, 0, 0),
    (1, 0, 0),
    (-1, 0, 0),
    (0, 1, 0),
    (0, -1, 0),
    (0, 0, 1),
    (0, 0, -1),
    (1, 1, 0),
    (-1, -1, 0),
    (1, -1, 0),
    (-1, 1, 0),
    (1, 0, 1),
    (-1, 0, -1),
    (1, 0, -1),
    (-1, 0, 1),
    (0, 1, 1),
    (0, -1, -1),
    (0, 1, -1),
    (0, -1, 1),
)
W = (1.0 / 3.0,) + (1.0 / 18.0,) * 6 + (1.0 / 36.0,) * 12
OPP = (0, 2, 1, 4, 3, 6, 5, 8, 7, 10, 9, 12, 11, 14, 13, 16, 15, 18, 17)
REACH = 4
PAD = 8
XR = (1, 7, 9, 11, 13)
XL = (2, 8, 10, 12, 14)
YU = (3, 7, 10, 15, 17)
YD = (4, 8, 9, 16, 18)
ZU = tuple(i for i in range(19) if C[i][2] == 1)
ZD = tuple(i for i in range(19) if C[i][2] == -1)
XS = XR + XL
STRIP = 80
BLK = 24


def cone(a, b):
    return max(0.0, 5.0 - math.sqrt(a * a + b * b))


def roll(v, shift, axis):
    size = v.shape[axis]
    if isinstance(shift, int):
        shift = shift % size
        if shift == 0:
            return v
    return pltpu.roll(v, shift, axis)


def lane_of(shape):
    return lax.broadcasted_iota(jnp.int32, shape, len(shape) - 1)


def row_of(shape):
    return lax.broadcasted_iota(jnp.int32, shape, len(shape) - 2)


def filtered(main, outer, tv):
    lane = lane_of((8, 128))
    sums = []
    for k in range(4):
        per_b = [main[k]]
        for b in range(1, REACH + 1):
            plus = jnp.where(lane < 128 - b, roll(main[k], -b, 1), roll(outer[k], -b, 1))
            minus = jnp.where(lane >= b, roll(main[k], b, 1), roll(outer[k], b, 1))
            per_b.append(plus + minus)
        sums.append(per_b)
    for a in range(REACH + 1):
        for k in range(4):
            total = None
            for b in range(REACH + 1):
                if cone(a, b) > 0.0:
                    term = cone(a, b) * sums[k][b]
                    total = term if total is None else total + term
            tv[a, 8 * k : 8 * k + 8, :] = total
    out = tv[0, 8:24, :]
    for a in range(1, REACH + 1):
        out = out + (tv[a, 8 - a : 24 - a, :] + tv[a, 8 + a : 24 + a, :])
    return out


def x_terms(pops, cm, cp, halves=(0, 1)):
    shape = (8, 128)
    lane, sub = lane_of(shape), row_of(shape)
    half = lane % 2
    block = lane // BLK
    ahead = roll(cp, -1, 0)
    ahead = jnp.where(sub < 7, ahead, jnp.where(half == 0, roll(ahead, -1, 1), 0.0))
    behind = roll(cp, 1, 0)
    behind = jnp.where(sub > 0, behind, jnp.where(half == 1, roll(behind, 1, 1), 0.0))
    src = cp
    for j in (1, 2):
        src = jnp.where(block == j, ahead if C[pops[j]][1] == 1 else behind, src)
    m0 = jnp.where(block == 0, cm, 0.0)
    m1 = jnp.where(block == 1, cm, 0.0)
    m2 = jnp.where(block == 2, cm, 0.0)
    u = m0
    for j in range(1, 5):
        u = u + roll(m0, BLK * j, 1)
    u = u * float(C[pops[0]][0])
    u = u + float(C[pops[1]][1]) * m1 + float(C[pops[2]][1]) * roll(m1, BLK, 1)
    u = u + float(C[pops[3]][2]) * roll(m2, BLK, 1) + float(C[pops[4]][2]) * roll(m2, 2 * BLK, 1)
    u = u * jnp.where(block == 0, 1.0 / 18.0, 1.0 / 36.0)
    prod = jnp.where(block < 5, u * src, 0.0)
    return [jnp.sum(jnp.where(half == h, prod, 0.0), axis=1, keepdims=True) for h in halves]


def strips(from_left, from_right, h):
    lane = lane_of((8, 128))
    a = roll(from_right, -(STRIP + 4 * h), 1)
    b = roll(from_left, 124 - (STRIP + 4 * h), 1)
    return jnp.where(lane < 4, a, jnp.where(lane >= 124, b, 0.0))


def shift_ext(main, outer, cx):
    if cx == 0:
        return main, outer
    lane = lane_of(main.shape)
    a, b = roll(main, -cx, 1), roll(outer, -cx, 1)
    edge = lane == (127 if cx == 1 else 0)
    return jnp.where(edge, b, a), jnp.where(edge, a, b)


def kernel(
    adj, mom, des, sol, por,
    new, sens,
    adjv, halo, momv, desv, solv, porv, mv, xs, yh, tv, den_v, ext,
    ym_s, ym_r, ya_s, ya_r, xb_s, xb_r, xg_r, nu_s, nu_r,
    in_sem, pl_s, pl_r, ym_ss, ym_rs, ya_ss, ya_rs, xb_ss, xb_rs, xg_ss, xg_rs, nu_ss, nu_rs,
    x_in, y_in, strong,
):
    gx, gy, core = lax.axis_index("gx"), lax.axis_index("gy"), lax.axis_index("depth")
    n_gx, n_gy = lax.axis_size("gx"), lax.axis_size("gy")
    has_x = (gx > 0, gx < n_gx - 1)
    has_y = (gy > 0, gy < n_gy - 1)
    to_x = ({"gx": gx - 1}, {"gx": gx + 1})
    to_y = ({"gy": gy - 1}, {"gy": gy + 1})
    to_p = {"depth": 1 - core}

    barrier = pltpu.get_barrier_semaphore()

    def tell(device):
        pl.semaphore_signal(barrier, inc=1, device_id=device, device_id_type=MESH)

    tell(to_p)
    for d in range(2):
        told = has_x[d] & (gx % 8 > 0) if d == 0 else has_x[d]
        pl.when(told)(functools.partial(tell, {**to_x[d], "depth": 0}))
        pl.when(has_y[d])(functools.partial(tell, {**to_y[d], "depth": 1}))

    def know(counter, other_sem, has):
        @pl.when(core == counter)
        def _():
            pl.semaphore_wait(barrier, 1 + 2 * sum(here.astype(jnp.int32) for here in has))
            pl.semaphore_signal(other_sem, inc=1, device_id=to_p, device_id_type=MESH)

        @pl.when(core != counter)
        def _():
            pl.semaphore_wait(other_sem, 1)

    know_x = functools.partial(know, 0, x_in, has_x)

    def know_y():
        know(1, y_in, has_y)
        pl.when(has_x[0] & (gx % 8 == 0))(functools.partial(tell, {**to_x[0], "depth": 0}))

    y_first = gx % 8 < 4
    x_first = jnp.logical_not(y_first)

    loads = [
        pltpu.make_async_copy(mom, momv, in_sem.at[19]),
        pltpu.make_async_copy(des, desv, in_sem.at[20]),
        pltpu.make_async_copy(sol, solv, in_sem.at[21]),
        pltpu.make_async_copy(por, porv, in_sem.at[22]),
    ]
    for i in range(19):
        start = PAD + (16 if C[i][2] == -1 else 0)
        loads.append(pltpu.make_async_copy(adj.at[i], adjv.at[i, pl.ds(start, 192), :], in_sem.at[i]))
    for copy in loads:
        copy.start()

    for d in range(2):

        def clear_x(d=d):
            xb_r[d] = jnp.zeros_like(xb_r[d])

        def clear_y(d=d):
            for ref in (ym_r, ya_r):
                ref[d] = jnp.zeros_like(ref[d])

        pl.when(jnp.logical_not(has_x[d]))(clear_x)
        pl.when(jnp.logical_not(has_y[d]))(clear_y)
        for e in range(2):

            def clear_xy(d=d, e=e):
                xg_r[2 * d + e] = jnp.zeros_like(xg_r[2 * d + e])

            pl.when(jnp.logical_not(has_x[d] & has_y[e]))(clear_xy)

    @pl.when(core == 0)
    def _():
        for i in ZD:
            adjv[i, PAD : PAD + 16, :] = jnp.zeros((16, 128), F32)

    @pl.when(core == 1)
    def _():
        for i in ZU:
            adjv[i, PAD + 192 : PAD + 208, :] = jnp.zeros((16, 128), F32)

    def planes(pops, src_row):
        return [
            pltpu.make_async_remote_copy(
                src_ref=adj.at[i, pl.ds(src_row, 16), :],
                dst_ref=halo.at[j],
                send_sem=pl_s.at[j],
                recv_sem=pl_r.at[j],
                device_id=to_p,
                device_id_type=MESH,
            )
            for j, i in enumerate(pops)
        ]

    plane_down = planes(ZD, 176)
    plane_up = planes(ZU, 0)

    def send_planes():
        @pl.when(core == 0)
        def _():
            for copy in plane_down:
                copy.start()

        @pl.when(core == 1)
        def _():
            for copy in plane_up:
                copy.start()

    @pl.when(x_first)
    def _():
        know_x()
        send_planes()

    def remote(src, dst, s_sem, r_sem, d, device):
        return pltpu.make_async_remote_copy(
            src_ref=src.at[d],
            dst_ref=dst.at[1 - d],
            send_sem=s_sem.at[d],
            recv_sem=r_sem.at[1 - d],
            device_id=device,
            device_id_type=MESH,
        )

    cxb = [remote(xb_s, xb_r, xb_ss, xb_rs, d, to_x[d]) for d in range(2)]
    cym = [remote(ym_s, ym_r, ym_ss, ym_rs, d, to_y[d]) for d in range(2)]
    cya = [remote(ya_s, ya_r, ya_ss, ya_rs, d, to_y[d]) for d in range(2)]
    cxg = [
        [
            pltpu.make_async_remote_copy(
                src_ref=xb_s.at[d],
                dst_ref=xg_r.at[2 * (1 - d) + 1 - e],
                send_sem=xg_ss.at[2 * d + e],
                recv_sem=xg_rs.at[2 * (1 - d) + 1 - e],
                device_id={**to_x[d], **to_y[e]},
                device_id_type=MESH,
            )
            for e in range(2)
        ]
        for d in range(2)
    ]
    cnu = pltpu.make_async_remote_copy(
        src_ref=nu_s, dst_ref=nu_r, send_sem=nu_ss.at[0], recv_sem=nu_rs.at[0], device_id=to_p, device_id_type=MESH
    )

    for copy in loads[:4]:
        copy.wait()

    slope3 = 3.0 / ((1.0 + desv[...]) * (1.0 + desv[...]))

    @pl.loop(0, 12)
    def _(z):
        rows = pl.ds(pl.multiple_of(z * 16, 16), 16)
        keep = (solv[rows, :] == 0) & (porv[rows, :] != 1)
        scale = jnp.where(keep, slope3, 0.0)
        for k in range(3):
            mv[k, rows, :] = scale * momv[k, rows, :]

    for copy in loads[4:]:
        copy.wait()

    zo = [PAD + (16 if C[i][2] == 1 else 0) for i in range(19)]
    lane12 = lane_of((12, 128))
    lane8 = lane_of((8, 128))

    def pack(d, z, cp, cm):
        edge = 127 if d == 1 else 0
        pops = XL if d == 1 else XR
        for h in range(2):
            row = pl.multiple_of(z * 16, 16) + 8 * h
            for j in range(5):
                here = lane8 == 2 * z + h + BLK * j
                v = adjv[pops[j], pl.ds(zo[pops[j]] + row, 8), :]
                cp = jnp.where(here, jnp.broadcast_to(v[:, edge : edge + 1], (8, 128)), cp)
                if j < 3:
                    m = mv[j, pl.ds(row, 8), :]
                    cm = jnp.where(here, jnp.broadcast_to(m[:, edge : edge + 1], (8, 128)), cm)
        return cp, cm

    lane16, row16 = lane_of((16, 128)), row_of((16, 128))

    def inner(z, total):
        base = pl.multiple_of(z * 16, 16)
        last, first = row16 == 15, row16 == 0

        def at(i):
            return adjv[i, pl.ds(zo[i] + base + C[i][1], 16), :]

        def up(v):
            return jnp.where(last, 0.0, v)

        def down(v):
            return jnp.where(first, 0.0, v)

        def right(v):
            return jnp.where(lane16 == 127, 0.0, roll(v, -1, 1))

        def left(v):
            return jnp.where(lane16 == 0, 0.0, roll(v, 1, 1))

        v7, v9, v8, v10 = up(at(7)), down(at(9)), down(at(8)), up(at(10))
        v11, v13, v12, v14 = at(11), at(13), at(12), at(14)
        x_sum = right((2.0 * at(1) + v7) + (v9 + v11) + v13) - left((2.0 * at(2) + v8) + (v10 + v12) + v14)
        v15, v17, v16, v18 = at(15), at(17), at(16), at(18)
        y_sum = up((2.0 * at(3) + v15) + v17) - down((2.0 * at(4) + v16) + v18)
        y_sum = y_sum + right(v7 - v9) + left(v10 - v8)
        z_sum = 2.0 * (at(5) - at(6)) + up(v15 - v17) + down(v18 - v16)
        z_sum = z_sum + right(v11 - v13) + left(v14 - v12)
        return (
            total
            + x_sum * mv[0, pl.ds(base, 16), :]
            + y_sum * mv[1, pl.ds(base, 16), :]
            + z_sum * mv[2, pl.ds(base, 16), :]
        )

    def both(z, carry):
        return (*pack(1, z, *carry[:2]), inner(z, carry[2]))

    zero8 = jnp.zeros((8, 128), F32)
    carry = lax.fori_loop(core, core + 11, both, (zero8, zero8, jnp.zeros((16, 128), F32)))

    @pl.when(y_first)
    def _():
        know_y()
        send_planes()

    @pl.when(core == 0)
    def _():
        for copy in plane_up:
            copy.wait_recv()
        for j, i in enumerate(ZU):
            adjv[i, PAD + 192 : PAD + 208, :] = halo[j]

    @pl.when(core == 1)
    def _():
        for copy in plane_down:
            copy.wait_recv()
        for j, i in enumerate(ZD):
            adjv[i, PAD : PAD + 16, :] = halo[j]

    cp1, cm1, a0 = both(11 * (1 - core), carry)
    a0 = a0 * (1.0 / 36.0)

    def with_strips(d, cm):
        for h in range(2):
            first = STRIP + 4 * h
            moved = roll(a0[8 * h : 8 * h + 8], first - (124 if d == 1 else 0), 1)
            cm = jnp.where((lane8 >= first) & (lane8 < first + 4), moved, cm)
        return cm

    xb_s[1, 0:8, :] = cp1
    xb_s[1, 8:16, :] = with_strips(1, cm1)

    edge_rows = []
    for d, (pops, row) in enumerate(((YU, 0), (YD, 15))):
        values = [adjv[i, pl.ds(zo[i] + row, 12, stride=16), :] for i in pops]
        values += [mv[k, pl.ds(row, 12, stride=16), :] for k in range(3)]
        edge_rows.append(values)
        for v in range(8):
            ym_s[d, v] = values[v]
    def pack_rows(d):
        packed = jnp.zeros((12, 128), F32)
        for l in range(2):
            for v in range(8):
                slot = 64 * l + 8 * v
                moved = roll(edge_rows[l][v], slot - (0 if d == 0 else 120), 1)
                packed = jnp.where((lane12 >= slot) & (lane12 < slot + 8), moved, packed)
        xb_s[d, 16:28, :] = packed

    def send_x(d):
        pl.when(has_x[d])(cxb[d].start)

    def send_xy(d, when):
        for e in range(2):
            pl.when(when & has_x[d] & has_y[e])(cxg[d][e].start)

    def send_y():
        for d in range(2):
            ya_s[d, 0:8, :] = a0[8 * d : 8 * d + 8]
            ya_s[d, 8:24, :] = xb_s[0, 0:16, :]
            ya_s[d, 24:40, :] = xb_s[1, 0:16, :]
            pl.when(has_y[d])(cym[d].start)
            pl.when(has_y[d])(cya[d].start)

    def tell_strong():
        for d in range(2):
            pl.when(has_x[d] & (gx % 8 > 0) if d == 0 else has_x[d])(
                functools.partial(pl.semaphore_signal, strong.at[1 - d], inc=1, device_id=to_x[d], device_id_type=MESH)
            )

    pack_rows(1)

    @pl.when(x_first)
    def _():
        send_x(1)
        send_xy(1, gx % 8 == 7)

    cp0, cm0 = lax.fori_loop(0, 12, lambda z, carry: pack(0, z, *carry), (zero8, zero8))
    xb_s[0, 0:8, :] = cp0
    xb_s[0, 8:16, :] = with_strips(0, cm0)
    pack_rows(0)

    @pl.when(y_first)
    def _():
        send_y()
        know_x()
        send_x(0)
        send_x(1)
        tell_strong()

    @pl.when(x_first)
    def _():
        send_x(0)
        know_y()
        send_y()
        tell_strong()

    @pl.when(has_x[1] & (gx % 8 < 7))
    def _():
        pl.semaphore_wait(strong.at[1], 1)
        send_xy(1, True)

    def send_left():
        pl.semaphore_wait(strong.at[0], 1)
        send_xy(0, True)

    pl.when(has_x[0] & (gx % 8 > 0))(send_left)

    row8 = row_of((8, 128))
    ones, ones_out = [], []
    for k in range(4):
        y = gy * 16 + (row8 + (8 * k - 8))
        inside = (y >= 0) & (y < 16 * n_gy)
        ones.append(jnp.where(inside, 1.0, 0.0))
        x_out = jnp.where(lane8 < 64, gx * 128 + 128 + lane8, gx * 128 - 128 + lane8)
        ones_out.append(jnp.where(inside & (x_out >= 0) & (x_out < 128 * n_gx), 1.0, 0.0))
    den_v[...] = filtered(ones, ones_out, tv)

    for d in range(2):
        pl.when(has_x[d])(cxb[1 - d].wait_recv)
    cp_l, cm_l, left = xb_r[0, 0:8, :], xb_r[0, 8:16, :], xb_r[0, 16:28, :]
    cp_r, cm_r, right = xb_r[1, 0:8, :], xb_r[1, 8:16, :], xb_r[1, 16:28, :]

    def with_x_terms(inside, near, far, halves):
        (np0, nm0, np1, nm1), (fp0, fm0, fp1, fm1) = near, far
        own = (x_terms(XL, nm0, fp0, halves), x_terms(XR, nm1, fp1, halves))
        theirs = (x_terms(XR, fm0, np0, halves), x_terms(XL, fm1, np1, halves))
        out = []
        for n, h in enumerate(halves):
            main = inside[n] + jnp.where(lane8 == 0, own[0][n], 0.0) + jnp.where(lane8 == 127, own[1][n], 0.0)
            outer = strips(fm0, fm1, h)
            outer = outer + jnp.where(lane8 == 127, theirs[0][n], 0.0) + jnp.where(lane8 == 0, theirs[1][n], 0.0)
            out.append([main, outer])
        return out

    blocks = with_x_terms([a0[0:8], a0[8:16]], (cp0, cm0, cp1, cm1), (cp_l, cm_l, cp_r, cm_r), (0, 1))

    def move(z, carry):
        for h in range(2):
            row = pl.multiple_of(z * 16, 16) + 8 * h
            for n, i in enumerate(XS):
                at = 2 * z + h + BLK * (n % 5)
                v = adjv[i, pl.ds(zo[i] + row, 8), :]
                if n < 5:
                    v = jnp.where(lane8 == 127, roll(cp_r, 127 - at, 1), roll(v, -1, 1))
                else:
                    v = jnp.where(lane8 == 0, roll(cp_l, 128 - at, 1), roll(v, 1, 1))
                xs[n, pl.ds(PAD + row, 8), :] = v
        return carry

    lax.fori_loop(0, 12, move, 0)

    def ends(from_right, from_left, at_right, at_left):
        a = roll(from_right, -at_right, 1)
        b = roll(from_left, 120 - at_left, 1)
        return jnp.where(lane12 < 8, a, jnp.where(lane12 >= 120, b, 0.0))

    own_outer = [[ends(right, left, 64 * l + 8 * v, 64 * l + 8 * v) for v in range(8)] for l in range(2)]

    pl.when(has_x[0] & (gx % 8 == 0))(send_left)

    for d in range(2):
        pl.when(has_y[d])(cym[1 - d].wait_recv)
        pl.when(has_y[d])(cya[1 - d].wait_recv)
    for d in range(2):
        for e in range(2):
            pl.when(has_x[d] & has_y[e])(cxg[1 - d][1 - e].wait_recv)

    def weighted(pops, moms, pulled):
        total = None
        for j, i in enumerate(pops):
            c = C[i]
            u = None
            for k in range(3):
                if c[k] != 0:
                    u = (moms[k] if c[k] == 1 else -moms[k]) if u is None else (u + moms[k] if c[k] == 1 else u - moms[k])
            term = (W[i] * u) * pulled[j]
            total = term if total is None else total + term
        return jnp.sum(total, axis=0, keepdims=True)

    inside_rows, beyond_rows = [], []
    for d, (mine, others) in enumerate(((YU, YD), (YD, YU))):
        got = [ym_r[d, v] for v in range(8)]
        slot = 64 * (1 - d)
        got_outer = [
            ends(xg_r[2 + d, 16:28, :], xg_r[d, 16:28, :], slot + 8 * v, slot + 8 * v) for v in range(8)
        ]
        moved = [shift_ext(got[j], got_outer[j], C[others[j]][0]) for j in range(5)]
        for j in range(5):
            yh[d, j] = moved[j][0]
        inside_rows.append(
            (
                weighted(others, edge_rows[d][5:], [m[0] for m in moved]),
                weighted(others, own_outer[d][5:], [m[1] for m in moved]),
            )
        )
        moved = [shift_ext(edge_rows[d][j], own_outer[d][j], C[mine[j]][0]) for j in range(5)]
        beyond_rows.append(
            (weighted(mine, got[5:], [m[0] for m in moved]), weighted(mine, got_outer[5:], [m[1] for m in moved]))
        )

    beyond = []
    for e in range(2):
        near = [ya_r[e, 8 + 8 * n : 16 + 8 * n, :] for n in range(4)]
        far = [xg_r[2 * d + e, 8 * n : 8 * n + 8, :] for d in range(2) for n in range(2)]
        beyond += with_x_terms([ya_r[e, 0:8, :]], near, far, (1 - e,))
    blocks = [beyond[0], *blocks, beyond[1]]
    for part in range(2):
        blocks[0][part] = blocks[0][part] + jnp.where(row8 == 7, beyond_rows[0][part], 0.0)
        blocks[1][part] = blocks[1][part] + jnp.where(row8 == 0, inside_rows[0][part], 0.0)
        blocks[2][part] = blocks[2][part] + jnp.where(row8 == 7, inside_rows[1][part], 0.0)
        blocks[3][part] = blocks[3][part] + jnp.where(row8 == 0, beyond_rows[1][part], 0.0)
    number = filtered([b[0] for b in blocks], [b[1] for b in blocks], tv)
    nu_s[...] = number
    cnu.start()

    damping = 0.5 * (1.0 - desv[...]) / (1.0 + desv[...])

    @pl.loop(0, 12)
    def _(z):
        base = pl.multiple_of(z * 16, 16)
        rows = pl.ds(base, 16)
        pulled = []
        for i in range(19):
            c = C[i]
            if c[0] != 0:
                v = xs[XS.index(i), pl.ds(PAD + base + c[1], 16), :]
            else:
                v = adjv[i, pl.ds(zo[i] + base + c[1], 16), :]
            if c[1] == 1:
                v = jnp.where(row16 == 15, yh[1, YU.index(i), pl.ds(z, 1), :], v)
            elif c[1] == -1:
                v = jnp.where(row16 == 0, yh[0, YD.index(i), pl.ds(z, 1), :], v)
            pulled.append(v)
        zeroth = W[0] * pulled[0]
        sums = [jnp.zeros((16, 128), F32)] * 3
        for i in range(1, 19):
            v = W[i] * pulled[i]
            zeroth = zeroth + v
            for k in range(3):
                if C[i][k] == 1:
                    sums[k] = sums[k] + v
                elif C[i][k] == -1:
                    sums[k] = sums[k] - v
        gain = (1.25 - damping) * 3.0
        sums = [gain * s for s in sums]
        base_term = 1.25 * zeroth
        fluid = solv[rows, :] == 0
        port = porv[rows, :]
        inlet, outlet = port == 1, port == 2
        bump = jnp.where(outlet, 1.0, 0.0)
        for i in range(19):
            c = C[i]
            relaxed = base_term - 0.25 * pulled[i]
            for k in range(3):
                if c[k] == 1:
                    relaxed = relaxed + sums[k]
                elif c[k] == -1:
                    relaxed = relaxed - sums[k]
            out = jnp.where(fluid, relaxed, pulled[OPP[i]])
            out = jnp.where(inlet, 0.0, out)
            if c[0] == 1:
                out = out + bump
            elif c[0] == -1:
                out = out - bump
            new[i, rows, :] = out

    cnu.wait_recv()
    sens[...] = (number + nu_r[...]) / den_v[...]

    @pl.when(core == 0)
    def _():
        for copy in plane_down:
            copy.wait_send()

    @pl.when(core == 1)
    def _():
        for copy in plane_up:
            copy.wait_send()

    for d in range(2):
        pl.when(has_x[d])(cxb[d].wait_send)
        for copy in (cym[d], cya[d]):
            pl.when(has_y[d])(copy.wait_send)
        for e in range(2):
            pl.when(has_x[d] & has_y[e])(cxg[d][e].wait_send)
    cnu.wait_send()


def write_out(new_v, sens_v, new, sens, sem):
    copies = [pltpu.make_async_copy(new_v.at[i], new.at[i], sem.at[i]) for i in range(19)]
    copies.append(pltpu.make_async_copy(sens_v, sens, sem.at[19]))
    for copy in copies:
        copy.start()
    for copy in copies:
        copy.wait()


def on_device(adjoint, momentum, design, solid_mask, port_label):
    hbm = pl.BlockSpec(memory_space=pl.ANY)
    vmem = pl.BlockSpec(memory_space=pltpu.VMEM)
    dma = pltpu.SemaphoreType.DMA
    v = lambda *shape, t=F32: pltpu.VMEM(shape, t)
    buffers = [
        v(19, 224, 128), v(5, 16, 128), v(3, 192, 128), v(16, 128), v(192, 128, t=jnp.int32), v(192, 128, t=jnp.int32),
        v(3, 192, 128), v(10, 208, 128), v(2, 5, 12, 128), v(5, 32, 128), v(16, 128), v(8, 128),
    ]
    for shape in ((8, 12, 128), (40, 128), (28, 128)):
        buffers += [v(2, *shape), v(2, *shape)]
    buffers += [v(4, 28, 128)]
    buffers += [v(16, 128), v(16, 128)]
    regular = pltpu.SemaphoreType.REGULAR
    sems = [dma((23,)), dma((5,)), dma((5,))] + [dma((2,))] * 6 + [dma((4,))] * 2 + [dma((1,))] * 2
    sems += [regular, regular, regular((2,))]
    new, sens = pl.pallas_call(
        kernel,
        out_shape=(v(19, 192, 128), v(16, 128)),
        in_specs=[hbm] * 5,
        out_specs=(vmem, vmem),
        scratch_shapes=buffers + sems,
        compiler_params=pltpu.CompilerParams(collective_id=0, has_side_effects=True),
    )(
        adjoint.reshape(19, 192, 128),
        momentum.reshape(3, 192, 128),
        design,
        solid_mask.reshape(192, 128),
        port_label.reshape(192, 128),
    )
    new, sens = pl.pallas_call(
        write_out,
        out_shape=(jax.ShapeDtypeStruct((19, 192, 128), F32), jax.ShapeDtypeStruct((16, 128), F32)),
        in_specs=[vmem, vmem],
        out_specs=(hbm, hbm),
        scratch_shapes=[dma((20,))],
    )(*(pltpu.with_memory_space_constraint(x, pltpu.VMEM) for x in (new, sens)))
    return new.reshape(19, 12, 16, 128), sens


def solution(mesh):
    cells = P("depth", "gy", "gx")
    fields = P(None, "depth", "gy", "gx")
    plane = P("gy", "gx")
    return jax.shard_map(
        on_device,
        mesh=mesh,
        in_specs=(fields, fields, plane, cells, cells),
        out_specs=(fields, plane),
        check_vma=False,
    )
```

```python
import functools
import math

import jax
import jax.numpy as jnp
from jax import lax
from jax.experimental import pallas as pl
from jax.experimental.pallas import tpu as pltpu
from jax.sharding import PartitionSpec as P

MESH = pl.DeviceIdType.MESH
F32 = jnp.float32
C = (
    (0, 0, 0),
    (1, 0, 0),
    (-1, 0, 0),
    (0, 1, 0),
    (0, -1, 0),
    (0, 0, 1),
    (0, 0, -1),
    (1, 1, 0),
    (-1, -1, 0),
    (1, -1, 0),
    (-1, 1, 0),
    (1, 0, 1),
    (-1, 0, -1),
    (1, 0, -1),
    (-1, 0, 1),
    (0, 1, 1),
    (0, -1, -1),
    (0, 1, -1),
    (0, -1, 1),
)
W = (1.0 / 3.0,) + (1.0 / 18.0,) * 6 + (1.0 / 36.0,) * 12
OPP = (0, 2, 1, 4, 3, 6, 5, 8, 7, 10, 9, 12, 11, 14, 13, 16, 15, 18, 17)
REACH = 4
PAD = 8
XR = (1, 7, 9, 11, 13)
XL = (2, 8, 10, 12, 14)
YU = (3, 7, 10, 15, 17)
YD = (4, 8, 9, 16, 18)
ZU = tuple(i for i in range(19) if C[i][2] == 1)
ZD = tuple(i for i in range(19) if C[i][2] == -1)
XS = XR + XL
STRIP = 80
BLK = 24


def cone(a, b):
    return max(0.0, 5.0 - math.sqrt(a * a + b * b))


def roll(v, shift, axis):
    size = v.shape[axis]
    if isinstance(shift, int):
        shift = shift % size
        if shift == 0:
            return v
    return pltpu.roll(v, shift, axis)


def lane_of(shape):
    return lax.broadcasted_iota(jnp.int32, shape, len(shape) - 1)


def row_of(shape):
    return lax.broadcasted_iota(jnp.int32, shape, len(shape) - 2)


def filtered(main, outer, tv):
    lane = lane_of((8, 128))
    sums = []
    for k in range(4):
        per_b = [main[k]]
        for b in range(1, REACH + 1):
            plus = jnp.where(lane < 128 - b, roll(main[k], -b, 1), roll(outer[k], -b, 1))
            minus = jnp.where(lane >= b, roll(main[k], b, 1), roll(outer[k], b, 1))
            per_b.append(plus + minus)
        sums.append(per_b)
    for a in range(REACH + 1):
        for k in range(4):
            total = None
            for b in range(REACH + 1):
                if cone(a, b) > 0.0:
                    term = cone(a, b) * sums[k][b]
                    total = term if total is None else total + term
            tv[a, 8 * k : 8 * k + 8, :] = total
    out = tv[0, 8:24, :]
    for a in range(1, REACH + 1):
        out = out + (tv[a, 8 - a : 24 - a, :] + tv[a, 8 + a : 24 + a, :])
    return out


def x_terms(pops, cm, cp, halves):
    shape = (8, 128)
    lane, sub = lane_of(shape), row_of(shape)
    half = lane % 2
    block = lane // BLK
    ahead, behind = roll(cp, -1, 0), roll(cp, 1, 0)
    if len(halves) == 2:
        ahead = jnp.where(sub < 7, ahead, jnp.where(half == 0, roll(ahead, -1, 1), 0.0))
        behind = jnp.where(sub > 0, behind, jnp.where(half == 1, roll(behind, 1, 1), 0.0))
    else:
        ahead, behind = jnp.where(sub < 7, ahead, 0.0), jnp.where(sub > 0, behind, 0.0)
    src = cp
    for j in (1, 2):
        src = jnp.where(block == j, ahead if C[pops[j]][1] == 1 else behind, src)
    m0 = jnp.where(block == 0, cm, 0.0)
    m1 = jnp.where(block == 1, cm, 0.0)
    m2 = jnp.where(block == 2, cm, 0.0)
    u = m0
    for j in range(1, 5):
        u = u + roll(m0, BLK * j, 1)
    u = u * float(C[pops[0]][0])
    u = u + float(C[pops[1]][1]) * m1 + float(C[pops[2]][1]) * roll(m1, BLK, 1)
    u = u + float(C[pops[3]][2]) * roll(m2, BLK, 1) + float(C[pops[4]][2]) * roll(m2, 2 * BLK, 1)
    u = u * jnp.where(block == 0, 1.0 / 18.0, 1.0 / 36.0)
    prod = jnp.where(block < 5, u * src, 0.0)
    return [jnp.sum(jnp.where(half == h, prod, 0.0), axis=1, keepdims=True) for h in halves]


def joined(cp, cm, h):
    lane = lane_of((8, 128))
    even = lane % 2 == 0
    both = jnp.where(even, cp, roll(cm, 1, 1)) if h == 0 else jnp.where(even, roll(cp, -1, 1), cm)
    near = roll(cm, 120 - (STRIP + 4 * h), 1)
    return jnp.where(lane < 120, both, jnp.where(lane < 124, near, 0.0))


def parted(both):
    lane = lane_of((8, 128))
    even = (lane % 2 == 0) & (lane < 120)
    return jnp.where(even, both, 0.0), jnp.where(even, roll(both, -1, 1), 0.0)


def strips(from_left, from_right, first):
    lane = lane_of((8, 128))
    a = roll(from_right, -first, 1)
    b = roll(from_left, 124 - first, 1)
    return jnp.where(lane < 4, a, jnp.where(lane >= 124, b, 0.0))


def shift_ext(main, outer, cx):
    if cx == 0:
        return main, outer
    lane = lane_of(main.shape)
    a, b = roll(main, -cx, 1), roll(outer, -cx, 1)
    edge = lane == (127 if cx == 1 else 0)
    return jnp.where(edge, b, a), jnp.where(edge, a, b)


def kernel(
    adj, mom, des, sol, por,
    new, sens,
    adjv, halo, momv, desv, solv, porv, mv, xs, yh, tv, den_v, ext,
    ym_s, ym_r, ya_s, ya_r, xb_s, xb_r, xg_s, xg_r, hop_r, rlx, nu_s, nu_r,
    in_sem, pl_s, pl_r, ym_ss, ym_rs, ya_ss, ya_rs, xb_ss, xb_rs, xg_ss, xg_rs, hop_ss, hop_rs, on_ss, nu_ss, nu_rs,
    x_in, y_in, left_in, strong,
):
    gx, gy, core = lax.axis_index("gx"), lax.axis_index("gy"), lax.axis_index("depth")
    n_gx, n_gy = lax.axis_size("gx"), lax.axis_size("gy")
    has_x = (gx > 0, gx < n_gx - 1)
    has_y = (gy > 0, gy < n_gy - 1)
    to_x = ({"gx": gx - 1}, {"gx": gx + 1})
    to_y = ({"gy": gy - 1}, {"gy": gy + 1})
    to_p = {"depth": 1 - core}

    barrier = pltpu.get_barrier_semaphore()

    def tell(device):
        pl.semaphore_signal(barrier, inc=1, device_id=device, device_id_type=MESH)

    tell(to_p)
    for d in range(2):
        told = has_x[d] & (gx % 8 > 0 if d == 0 else gx % 8 < 7)
        pl.when(told)(functools.partial(tell, {**to_x[d], "depth": 0}))
        pl.when(has_y[d])(functools.partial(tell, {**to_y[d], "depth": 1}))

    def know(counter, other_sem, has):
        @pl.when(core == counter)
        def _():
            pl.semaphore_wait(barrier, 1 + 2 * sum(one.astype(jnp.int32) for one in has))
            pl.semaphore_signal(other_sem, inc=1, device_id=to_p, device_id_type=MESH)

        @pl.when(core != counter)
        def _():
            pl.semaphore_wait(other_sem, 1)

    early, late = has_x[0] & (gx % 8 == 0), has_x[1] & (gx % 8 == 7)

    def know_x():
        know(0, x_in, (has_x[0] & (gx % 8 > 0), has_x[1]))

        @pl.when(late)
        def _():
            pl.semaphore_signal(left_in, inc=1, device_id=to_x[1], device_id_type=MESH)


    def know_y():
        know(1, y_in, has_y)
        pl.when(early)(functools.partial(tell, {**to_x[0], "depth": 0}))

    loads = [
        pltpu.make_async_copy(mom, momv, in_sem.at[19]),
        pltpu.make_async_copy(des, desv, in_sem.at[20]),
        pltpu.make_async_copy(sol, solv, in_sem.at[21]),
        pltpu.make_async_copy(por, porv, in_sem.at[22]),
    ]
    for i in range(19):
        start = PAD + (16 if C[i][2] == -1 else 0)
        loads.append(pltpu.make_async_copy(adj.at[i], adjv.at[i, pl.ds(start, 192), :], in_sem.at[i]))
    for copy in loads:
        copy.start()

    for d in range(2):

        def clear_x(d=d):
            xb_r[d] = jnp.zeros_like(xb_r[d])

        def clear_y(d=d):
            for ref in (ym_r, ya_r):
                ref[d] = jnp.zeros_like(ref[d])

        pl.when(jnp.logical_not(has_x[d]))(clear_x)
        pl.when(jnp.logical_not(has_y[d]))(clear_y)
        for e in range(2):

            def clear_xy(d=d, e=e):
                xg_r[2 * d + e] = jnp.zeros_like(xg_r[2 * d + e])

            pl.when(jnp.logical_not(has_x[d] & has_y[e]))(clear_xy)

    @pl.when(core == 0)
    def _():
        for i in ZD:
            adjv[i, PAD : PAD + 16, :] = jnp.zeros((16, 128), F32)

    @pl.when(core == 1)
    def _():
        for i in ZU:
            adjv[i, PAD + 192 : PAD + 208, :] = jnp.zeros((16, 128), F32)

    def planes(pops, src_row):
        return [
            pltpu.make_async_remote_copy(
                src_ref=adj.at[i, pl.ds(src_row, 16), :],
                dst_ref=halo.at[j],
                send_sem=pl_s.at[j],
                recv_sem=pl_r.at[j],
                device_id=to_p,
                device_id_type=MESH,
            )
            for j, i in enumerate(pops)
        ]

    plane_down = planes(ZD, 176)
    plane_up = planes(ZU, 0)

    def send_planes():
        @pl.when(core == 0)
        def _():
            for copy in plane_down:
                copy.start()

        @pl.when(core == 1)
        def _():
            for copy in plane_up:
                copy.start()

    know_x()
    send_planes()

    def remote(src, dst, s_sem, r_sem, d, device):
        return pltpu.make_async_remote_copy(
            src_ref=src.at[d] if src is not xb_s else src.at[d, pl.ds(0, 28), :],
            dst_ref=dst.at[1 - d],
            send_sem=s_sem.at[d],
            recv_sem=r_sem.at[1 - d],
            device_id=device,
            device_id_type=MESH,
        )

    cxb = [remote(xb_s, xb_r, xb_ss, xb_rs, d, to_x[d]) for d in range(2)]
    cym = [remote(ym_s, ym_r, ym_ss, ym_rs, d, to_y[d]) for d in range(2)]
    cya = [remote(ya_s, ya_r, ya_ss, ya_rs, d, to_y[d]) for d in range(2)]
    cxg = [
        [
            pltpu.make_async_remote_copy(
                src_ref=xg_s.at[2 * d + e],
                dst_ref=xg_r.at[2 * (1 - d) + 1 - e],
                send_sem=xg_ss.at[2 * d + e],
                recv_sem=xg_rs.at[2 * (1 - d) + 1 - e],
                device_id={**to_x[d], **to_y[e]},
                device_id_type=MESH,
            )
            for e in range(2)
        ]
        for d in range(2)
    ]
    hop = [
        pltpu.make_async_remote_copy(
            src_ref=xg_s.at[e],
            dst_ref=hop_r.at[e],
            send_sem=hop_ss.at[e],
            recv_sem=hop_rs.at[e],
            device_id=to_x[0],
            device_id_type=MESH,
        )
        for e in range(2)
    ]
    onward = [
        pltpu.make_async_remote_copy(
            src_ref=hop_r.at[e],
            dst_ref=xg_r.at[3 - e],
            send_sem=on_ss.at[e],
            recv_sem=xg_rs.at[3 - e],
            device_id=to_y[e],
            device_id_type=MESH,
        )
        for e in range(2)
    ]
    cnu = pltpu.make_async_remote_copy(
        src_ref=nu_s, dst_ref=nu_r, send_sem=nu_ss.at[0], recv_sem=nu_rs.at[0], device_id=to_p, device_id_type=MESH
    )

    for copy in loads[:4]:
        copy.wait()

    slope3 = 3.0 / ((1.0 + desv[...]) * (1.0 + desv[...]))

    @pl.loop(0, 12)
    def _(z):
        rows = pl.ds(pl.multiple_of(z * 16, 16), 16)
        keep = (solv[rows, :] == 0) & (porv[rows, :] != 1)
        scale = jnp.where(keep, slope3, 0.0)
        for k in range(3):
            mv[k, rows, :] = scale * momv[k, rows, :]

    for copy in loads[4:]:
        copy.wait()

    zo = [PAD + (16 if C[i][2] == 1 else 0) for i in range(19)]
    lane12 = lane_of((12, 128))
    lane8 = lane_of((8, 128))

    def pack(d, z, cp, cm):
        edge = 127 if d == 1 else 0
        pops = XL if d == 1 else XR
        for h in range(2):
            row = pl.multiple_of(z * 16, 16) + 8 * h
            for j in range(5):
                here = lane8 == 2 * z + h + BLK * j
                v = adjv[pops[j], pl.ds(zo[pops[j]] + row, 8), :]
                cp = jnp.where(here, jnp.broadcast_to(v[:, edge : edge + 1], (8, 128)), cp)
                if j < 3:
                    m = mv[j, pl.ds(row, 8), :]
                    cm = jnp.where(here, jnp.broadcast_to(m[:, edge : edge + 1], (8, 128)), cm)
        return cp, cm

    lane16, row16 = lane_of((16, 128)), row_of((16, 128))

    def inner(z, total):
        base = pl.multiple_of(z * 16, 16)
        last, first = row16 == 15, row16 == 0

        def at(i):
            return adjv[i, pl.ds(zo[i] + base + C[i][1], 16), :]

        def up(v):
            return jnp.where(last, 0.0, v)

        def down(v):
            return jnp.where(first, 0.0, v)

        def right(v):
            return jnp.where(lane16 == 127, 0.0, roll(v, -1, 1))

        def left(v):
            return jnp.where(lane16 == 0, 0.0, roll(v, 1, 1))

        v7, v9, v8, v10 = up(at(7)), down(at(9)), down(at(8)), up(at(10))
        v11, v13, v12, v14 = at(11), at(13), at(12), at(14)
        x_sum = right((2.0 * at(1) + v7) + (v9 + v11) + v13) - left((2.0 * at(2) + v8) + (v10 + v12) + v14)
        v15, v17, v16, v18 = at(15), at(17), at(16), at(18)
        y_sum = up((2.0 * at(3) + v15) + v17) - down((2.0 * at(4) + v16) + v18)
        y_sum = y_sum + right(v7 - v9) + left(v10 - v8)
        z_sum = 2.0 * (at(5) - at(6)) + up(v15 - v17) + down(v18 - v16)
        z_sum = z_sum + right(v11 - v13) + left(v14 - v12)
        return (
            total
            + x_sum * mv[0, pl.ds(base, 16), :]
            + y_sum * mv[1, pl.ds(base, 16), :]
            + z_sum * mv[2, pl.ds(base, 16), :]
        )

    def both(z, carry):
        return (*pack(1, z, *carry[:2]), inner(z, carry[2]))

    zero8 = jnp.zeros((8, 128), F32)
    carry = lax.fori_loop(core, core + 11, both, (zero8, zero8, jnp.zeros((16, 128), F32)))

    @pl.when(core == 0)
    def _():
        for copy in plane_up:
            copy.wait_recv()
        for j, i in enumerate(ZU):
            adjv[i, PAD + 192 : PAD + 208, :] = halo[j]

    @pl.when(core == 1)
    def _():
        for copy in plane_down:
            copy.wait_recv()
        for j, i in enumerate(ZD):
            adjv[i, PAD : PAD + 16, :] = halo[j]

    cp1, cm1, a0 = both(11 * (1 - core), carry)
    a0 = a0 * (1.0 / 36.0)

    def with_strips(d, cm):
        for h in range(2):
            first = STRIP + 4 * h
            moved = roll(a0[8 * h : 8 * h + 8], first - (124 if d == 1 else 0), 1)
            cm = jnp.where((lane8 >= first) & (lane8 < first + 4), moved, cm)
        return cm

    xb_s[1, 0:8, :] = cp1
    xb_s[1, 8:16, :] = with_strips(1, cm1)

    edge_rows = []
    for d, (pops, row) in enumerate(((YU, 0), (YD, 15))):
        values = [adjv[i, pl.ds(zo[i] + row, 12, stride=16), :] for i in pops]
        values += [mv[k, pl.ds(row, 12, stride=16), :] for k in range(3)]
        edge_rows.append(values)
        for v in range(8):
            ym_s[d, v] = values[v]
    def pack_rows(d):
        packed = jnp.zeros((12, 128), F32)
        for l in range(2):
            for v in range(8):
                slot = 64 * l + 8 * v
                moved = roll(edge_rows[l][v], slot - (0 if d == 0 else 120), 1)
                packed = jnp.where((lane12 >= slot) & (lane12 < slot + 8), moved, packed)
        xb_s[d, 16:28, :] = packed

    def pack_corners(d):
        head, tail = xb_s[d, 16:24, :], xb_s[d, 24:32, :]
        for e in range(2):
            xg_s[2 * d + e, 0:8, :] = joined(xb_s[d, 0:8, :], xb_s[d, 8:16, :], e)
            if e == 0:
                xg_s[2 * d + e, 8:16, :] = jnp.where(lane8 < 64, head, roll(tail, 64, 1))
            else:
                xg_s[2 * d + e, 8:16, :] = jnp.where(lane8 < 64, roll(head, 64, 1), tail)

    def send_x(d):
        pl.when(has_x[d])(cxb[d].start)

    def send_xy(d, when):
        for e in range(2):
            pl.when(when & has_x[d] & has_y[e])(cxg[d][e].start)

    def send_y():
        for d in range(2):
            ya_s[d, 0:8, :] = a0[8 * d : 8 * d + 8]
            ya_s[d, 8:16, :] = xg_s[d, 0:8, :]
            ya_s[d, 16:24, :] = xg_s[2 + d, 0:8, :]
            pl.when(has_y[d])(cym[d].start)
            pl.when(has_y[d])(cya[d].start)

    def tell_strong():
        for d in range(2):
            pl.when(has_x[d] & (gx % 8 > 0 if d == 0 else gx % 8 < 7))(
                functools.partial(pl.semaphore_signal, strong.at[1 - d], inc=1, device_id=to_x[d], device_id_type=MESH)
            )

    for d in range(2):
        xb_s[d, 24:32, :] = zero8
    pack_rows(1)
    pack_corners(1)

    send_x(1)
    send_xy(1, late)

    cp0, cm0 = lax.fori_loop(0, 12, lambda z, carry: pack(0, z, *carry), (zero8, zero8))
    xb_s[0, 0:8, :] = cp0
    xb_s[0, 8:16, :] = with_strips(0, cm0)
    pack_rows(0)
    pack_corners(0)

    pl.when(jnp.logical_not(early))(functools.partial(send_x, 0))
    know_y()
    send_y()
    tell_strong()

    def send_left():
        pl.semaphore_wait(strong.at[0], 1)
        send_xy(0, True)

    def send_right():
        pl.semaphore_wait(strong.at[1], 1)
        send_xy(1, True)

    pl.when(has_x[0] & (gx % 8 > 1))(send_left)
    pl.when(has_x[1] & (gx % 8 < 7))(send_right)
    pl.when(has_x[0] & (gx % 8 == 1))(send_left)

    for e in range(2):

        @pl.when(late & has_y[e])
        def _(e=e):
            hop[e].wait_recv()
            onward[e].start()

    @pl.when(early)
    def _():
        pl.semaphore_wait(left_in, 1)
        send_x(0)
        for e in range(2):
            pl.when(has_y[e])(hop[e].start)

    row8 = row_of((8, 128))
    ones, ones_out = [], []
    for k in range(4):
        y = gy * 16 + (row8 + (8 * k - 8))
        inside = (y >= 0) & (y < 16 * n_gy)
        ones.append(jnp.where(inside, 1.0, 0.0))
        x_out = jnp.where(lane8 < 64, gx * 128 + 128 + lane8, gx * 128 - 128 + lane8)
        ones_out.append(jnp.where(inside & (x_out >= 0) & (x_out < 128 * n_gx), 1.0, 0.0))
    den_v[...] = filtered(ones, ones_out, tv)

    for d in range(2):
        pl.when(has_x[d])(cxb[1 - d].wait_recv)
    cp_l, cm_l, left = xb_r[0, 0:8, :], xb_r[0, 8:16, :], xb_r[0, 16:28, :]
    cp_r, cm_r, right = xb_r[1, 0:8, :], xb_r[1, 8:16, :], xb_r[1, 16:28, :]

    def with_x_terms(inside, near, far, ends_of, halves):
        (np0, nm0, np1, nm1), (fp0, fm0, fp1, fm1) = near, far
        own = (x_terms(XL, nm0, fp0, halves), x_terms(XR, nm1, fp1, halves))
        theirs = (x_terms(XR, fm0, np0, halves), x_terms(XL, fm1, np1, halves))
        out = []
        for n, h in enumerate(halves):
            main = inside[n] + jnp.where(lane8 == 0, own[0][n], 0.0) + jnp.where(lane8 == 127, own[1][n], 0.0)
            outer = ends_of[n]
            outer = outer + jnp.where(lane8 == 127, theirs[0][n], 0.0) + jnp.where(lane8 == 0, theirs[1][n], 0.0)
            out.append([main, outer])
        return out

    blocks = with_x_terms([a0[0:8], a0[8:16]], (cp0, cm0, cp1, cm1), (cp_l, cm_l, cp_r, cm_r), [strips(cm_l, cm_r, STRIP + 4 * h) for h in range(2)], (0, 1))

    def move(z, carry):
        for h in range(2):
            row = pl.multiple_of(z * 16, 16) + 8 * h
            for n, i in enumerate(XS):
                at = 2 * z + h + BLK * (n % 5)
                v = adjv[i, pl.ds(zo[i] + row, 8), :]
                if n < 5:
                    v = jnp.where(lane8 == 127, roll(cp_r, 127 - at, 1), roll(v, -1, 1))
                else:
                    v = jnp.where(lane8 == 0, roll(cp_l, 128 - at, 1), roll(v, 1, 1))
                xs[n, pl.ds(PAD + row, 8), :] = v
        return carry

    lax.fori_loop(0, 12, move, 0)

    def ends(from_right, from_left, at_right, at_left):
        a = roll(from_right, -at_right, 1)
        b = roll(from_left, 120 - at_left, 1)
        return jnp.where(lane12 < 8, a, jnp.where(lane12 >= 120, b, 0.0))

    own_outer = [[ends(right, left, 64 * l + 8 * v, 64 * l + 8 * v) for v in range(8)] for l in range(2)]

    for d in range(2):
        pl.when(has_y[d])(cym[1 - d].wait_recv)
        pl.when(has_y[d])(cya[1 - d].wait_recv)
    for d in range(2):
        for e in range(2):
            pl.when(has_x[d] & has_y[e])(cxg[1 - d][1 - e].wait_recv)

    def weighted(pops, moms, pulled):
        total = None
        for j, i in enumerate(pops):
            c = C[i]
            u = None
            for k in range(3):
                if c[k] != 0:
                    u = (moms[k] if c[k] == 1 else -moms[k]) if u is None else (u + moms[k] if c[k] == 1 else u - moms[k])
            term = (W[i] * u) * pulled[j]
            total = term if total is None else total + term
        return jnp.sum(total, axis=0, keepdims=True)

    for n in range(4):
        rlx[n, 0:8, :] = xg_r[n, 8:16, :]
        rlx[n, 8:16, :] = roll(xg_r[n, 8:16, :], 64, 1)
    inside_rows, beyond_rows = [], []
    for d, (mine, others) in enumerate(((YU, YD), (YD, YU))):
        got = [ym_r[d, v] for v in range(8)]
        far_left, far_right = rlx[d, 0:12, :], rlx[2 + d, 0:12, :]
        got_outer = [ends(far_right, far_left, 8 * v, 8 * v) for v in range(8)]
        moved = [shift_ext(got[j], got_outer[j], C[others[j]][0]) for j in range(5)]
        for j in range(5):
            yh[d, j] = moved[j][0]
        inside_rows.append(
            (
                weighted(others, edge_rows[d][5:], [m[0] for m in moved]),
                weighted(others, own_outer[d][5:], [m[1] for m in moved]),
            )
        )
        moved = [shift_ext(edge_rows[d][j], own_outer[d][j], C[mine[j]][0]) for j in range(5)]
        beyond_rows.append(
            (weighted(mine, got[5:], [m[0] for m in moved]), weighted(mine, got_outer[5:], [m[1] for m in moved]))
        )

    beyond = []
    for e in range(2):
        near = (*parted(ya_r[e, 8:16, :]), *parted(ya_r[e, 16:24, :]))
        got_l, got_r = xg_r[e, 0:8, :], xg_r[2 + e, 0:8, :]
        far = (*parted(got_l), *parted(got_r))
        beyond += with_x_terms([ya_r[e, 0:8, :]], near, far, [strips(got_l, got_r, 120)], (0,))
    blocks = [beyond[0], *blocks, beyond[1]]
    for part in range(2):
        blocks[0][part] = blocks[0][part] + jnp.where(row8 == 7, beyond_rows[0][part], 0.0)
        blocks[1][part] = blocks[1][part] + jnp.where(row8 == 0, inside_rows[0][part], 0.0)
        blocks[2][part] = blocks[2][part] + jnp.where(row8 == 7, inside_rows[1][part], 0.0)
        blocks[3][part] = blocks[3][part] + jnp.where(row8 == 0, beyond_rows[1][part], 0.0)
    number = filtered([b[0] for b in blocks], [b[1] for b in blocks], tv)
    nu_s[...] = number
    cnu.start()

    damping = 0.5 * (1.0 - desv[...]) / (1.0 + desv[...])

    @pl.loop(0, 12)
    def _(z):
        base = pl.multiple_of(z * 16, 16)
        rows = pl.ds(base, 16)
        pulled = []
        for i in range(19):
            c = C[i]
            if c[0] != 0:
                v = xs[XS.index(i), pl.ds(PAD + base + c[1], 16), :]
            else:
                v = adjv[i, pl.ds(zo[i] + base + c[1], 16), :]
            if c[1] == 1:
                v = jnp.where(row16 == 15, yh[1, YU.index(i), pl.ds(z, 1), :], v)
            elif c[1] == -1:
                v = jnp.where(row16 == 0, yh[0, YD.index(i), pl.ds(z, 1), :], v)
            pulled.append(v)
        zeroth = W[0] * pulled[0]
        sums = [jnp.zeros((16, 128), F32)] * 3
        for i in range(1, 19):
            v = W[i] * pulled[i]
            zeroth = zeroth + v
            for k in range(3):
                if C[i][k] == 1:
                    sums[k] = sums[k] + v
                elif C[i][k] == -1:
                    sums[k] = sums[k] - v
        gain = (1.25 - damping) * 3.0
        sums = [gain * s for s in sums]
        base_term = 1.25 * zeroth
        fluid = solv[rows, :] == 0
        port = porv[rows, :]
        inlet, outlet = port == 1, port == 2
        bump = jnp.where(outlet, 1.0, 0.0)
        for i in range(19):
            c = C[i]
            relaxed = base_term - 0.25 * pulled[i]
            for k in range(3):
                if c[k] == 1:
                    relaxed = relaxed + sums[k]
                elif c[k] == -1:
                    relaxed = relaxed - sums[k]
            out = jnp.where(fluid, relaxed, pulled[OPP[i]])
            out = jnp.where(inlet, 0.0, out)
            if c[0] == 1:
                out = out + bump
            elif c[0] == -1:
                out = out - bump
            new[i, rows, :] = out

    cnu.wait_recv()
    sens[...] = (number + nu_r[...]) / den_v[...]

    @pl.when(core == 0)
    def _():
        for copy in plane_down:
            copy.wait_send()

    @pl.when(core == 1)
    def _():
        for copy in plane_up:
            copy.wait_send()

    for d in range(2):
        pl.when(has_x[d])(cxb[d].wait_send)
        for copy in (cym[d], cya[d]):
            pl.when(has_y[d])(copy.wait_send)
        for e in range(2):
            direct = has_x[d] & has_y[e] & (gx % 8 > 0) if d == 0 else has_x[d] & has_y[e]
            pl.when(direct)(cxg[d][e].wait_send)
        pl.when(early & has_y[d])(hop[d].wait_send)
        pl.when(late & has_y[d])(onward[d].wait_send)
    cnu.wait_send()


def write_out(new_v, sens_v, new, sens, sem):
    copies = [pltpu.make_async_copy(new_v.at[i], new.at[i], sem.at[i]) for i in range(19)]
    copies.append(pltpu.make_async_copy(sens_v, sens, sem.at[19]))
    for copy in copies:
        copy.start()
    for copy in copies:
        copy.wait()


def on_device(adjoint, momentum, design, solid_mask, port_label):
    hbm = pl.BlockSpec(memory_space=pl.ANY)
    vmem = pl.BlockSpec(memory_space=pltpu.VMEM)
    dma = pltpu.SemaphoreType.DMA
    v = lambda *shape, t=F32: pltpu.VMEM(shape, t)
    buffers = [
        v(19, 224, 128), v(5, 16, 128), v(3, 192, 128), v(16, 128), v(192, 128, t=jnp.int32), v(192, 128, t=jnp.int32),
        v(3, 192, 128), v(10, 208, 128), v(2, 5, 12, 128), v(5, 32, 128), v(16, 128), v(8, 128),
    ]
    buffers += [v(2, 8, 12, 128), v(2, 8, 12, 128), v(2, 24, 128), v(2, 24, 128), v(2, 32, 128), v(2, 28, 128)]
    buffers += [v(4, 16, 128), v(4, 16, 128), v(2, 16, 128), v(4, 16, 128)]
    buffers += [v(16, 128), v(16, 128)]
    regular = pltpu.SemaphoreType.REGULAR
    sems = [dma((23,)), dma((5,)), dma((5,))] + [dma((2,))] * 6 + [dma((4,))] * 2 + [dma((2,))] * 3 + [dma((1,))] * 2
    sems += [regular, regular, regular, regular((2,))]
    new, sens = pl.pallas_call(
        kernel,
        out_shape=(v(19, 192, 128), v(16, 128)),
        in_specs=[hbm] * 5,
        out_specs=(vmem, vmem),
        scratch_shapes=buffers + sems,
        compiler_params=pltpu.CompilerParams(collective_id=0, has_side_effects=True),
    )(
        adjoint.reshape(19, 192, 128),
        momentum.reshape(3, 192, 128),
        design,
        solid_mask.reshape(192, 128),
        port_label.reshape(192, 128),
    )
    new, sens = pl.pallas_call(
        write_out,
        out_shape=(jax.ShapeDtypeStruct((19, 192, 128), F32), jax.ShapeDtypeStruct((16, 128), F32)),
        in_specs=[vmem, vmem],
        out_specs=(hbm, hbm),
        scratch_shapes=[dma((20,))],
    )(*(pltpu.with_memory_space_constraint(x, pltpu.VMEM) for x in (new, sens)))
    return new.reshape(19, 12, 16, 128), sens


def solution(mesh):
    cells = P("depth", "gy", "gx")
    fields = P(None, "depth", "gy", "gx")
    plane = P("gy", "gx")
    return jax.shard_map(
        on_device,
        mesh=mesh,
        in_specs=(fields, fields, plane, cells, cells),
        out_specs=(fields, plane),
        check_vma=False,
    )
```

```python
import functools
import math

import jax
import jax.numpy as jnp
from jax import lax
from jax.experimental import pallas as pl
from jax.experimental.pallas import tpu as pltpu
from jax.sharding import PartitionSpec as P

MESH = pl.DeviceIdType.MESH
F32 = jnp.float32
C = (
    (0, 0, 0),
    (1, 0, 0),
    (-1, 0, 0),
    (0, 1, 0),
    (0, -1, 0),
    (0, 0, 1),
    (0, 0, -1),
    (1, 1, 0),
    (-1, -1, 0),
    (1, -1, 0),
    (-1, 1, 0),
    (1, 0, 1),
    (-1, 0, -1),
    (1, 0, -1),
    (-1, 0, 1),
    (0, 1, 1),
    (0, -1, -1),
    (0, 1, -1),
    (0, -1, 1),
)
W = (1.0 / 3.0,) + (1.0 / 18.0,) * 6 + (1.0 / 36.0,) * 12
OPP = (0, 2, 1, 4, 3, 6, 5, 8, 7, 10, 9, 12, 11, 14, 13, 16, 15, 18, 17)
REACH = 4
PAD = 8
XR = (1, 7, 9, 11, 13)
XL = (2, 8, 10, 12, 14)
YU = (3, 7, 10, 15, 17)
YD = (4, 8, 9, 16, 18)
ZU = tuple(i for i in range(19) if C[i][2] == 1)
ZD = tuple(i for i in range(19) if C[i][2] == -1)
XS = XR + XL
STRIP = 80
BLK = 24


def cone(a, b):
    return max(0.0, 5.0 - math.sqrt(a * a + b * b))


def roll(v, shift, axis):
    size = v.shape[axis]
    if isinstance(shift, int):
        shift = shift % size
        if shift == 0:
            return v
    return pltpu.roll(v, shift, axis)


def lane_of(shape):
    return lax.broadcasted_iota(jnp.int32, shape, len(shape) - 1)


def row_of(shape):
    return lax.broadcasted_iota(jnp.int32, shape, len(shape) - 2)


def filtered(main, outer, tv):
    lane = lane_of((8, 128))
    sums = []
    for k in range(4):
        per_b = [main[k]]
        for b in range(1, REACH + 1):
            plus = jnp.where(lane < 128 - b, roll(main[k], -b, 1), roll(outer[k], -b, 1))
            minus = jnp.where(lane >= b, roll(main[k], b, 1), roll(outer[k], b, 1))
            per_b.append(plus + minus)
        sums.append(per_b)
    for a in range(REACH + 1):
        for k in range(4):
            total = None
            for b in range(REACH + 1):
                if cone(a, b) > 0.0:
                    term = cone(a, b) * sums[k][b]
                    total = term if total is None else total + term
            tv[a, 8 * k : 8 * k + 8, :] = total
    out = tv[0, 8:24, :]
    for a in range(1, REACH + 1):
        out = out + (tv[a, 8 - a : 24 - a, :] + tv[a, 8 + a : 24 + a, :])
    return out


def x_terms(pops, cm, cp, halves):
    shape = (8, 128)
    lane, sub = lane_of(shape), row_of(shape)
    half = lane % 2
    block = lane // BLK
    ahead, behind = roll(cp, -1, 0), roll(cp, 1, 0)
    if len(halves) == 2:
        ahead = jnp.where(sub < 7, ahead, jnp.where(half == 0, roll(ahead, -1, 1), 0.0))
        behind = jnp.where(sub > 0, behind, jnp.where(half == 1, roll(behind, 1, 1), 0.0))
    else:
        ahead, behind = jnp.where(sub < 7, ahead, 0.0), jnp.where(sub > 0, behind, 0.0)
    src = cp
    for j in (1, 2):
        src = jnp.where(block == j, ahead if C[pops[j]][1] == 1 else behind, src)
    m0 = jnp.where(block == 0, cm, 0.0)
    m1 = jnp.where(block == 1, cm, 0.0)
    m2 = jnp.where(block == 2, cm, 0.0)
    u = m0
    for j in range(1, 5):
        u = u + roll(m0, BLK * j, 1)
    u = u * float(C[pops[0]][0])
    u = u + float(C[pops[1]][1]) * m1 + float(C[pops[2]][1]) * roll(m1, BLK, 1)
    u = u + float(C[pops[3]][2]) * roll(m2, BLK, 1) + float(C[pops[4]][2]) * roll(m2, 2 * BLK, 1)
    u = u * jnp.where(block == 0, 1.0 / 18.0, 1.0 / 36.0)
    prod = jnp.where(block < 5, u * src, 0.0)
    return [jnp.sum(jnp.where(half == h, prod, 0.0), axis=1, keepdims=True) for h in halves]


def joined(cp, cm, h):
    lane = lane_of((8, 128))
    even = lane % 2 == 0
    both = jnp.where(even, cp, roll(cm, 1, 1)) if h == 0 else jnp.where(even, roll(cp, -1, 1), cm)
    near = roll(cm, 120 - (STRIP + 4 * h), 1)
    return jnp.where(lane < 120, both, jnp.where(lane < 124, near, 0.0))


def parted(both):
    lane = lane_of((8, 128))
    even = (lane % 2 == 0) & (lane < 120)
    return jnp.where(even, both, 0.0), jnp.where(even, roll(both, -1, 1), 0.0)


def strips(from_left, from_right, first):
    lane = lane_of((8, 128))
    a = roll(from_right, -first, 1)
    b = roll(from_left, 124 - first, 1)
    return jnp.where(lane < 4, a, jnp.where(lane >= 124, b, 0.0))


def shift_ext(main, outer, cx):
    if cx == 0:
        return main, outer
    lane = lane_of(main.shape)
    a, b = roll(main, -cx, 1), roll(outer, -cx, 1)
    edge = lane == (127 if cx == 1 else 0)
    return jnp.where(edge, b, a), jnp.where(edge, a, b)


def kernel(
    adj, mom, des, sol, por,
    new, sens,
    adjv, halo, momv, desv, solv, porv, mv, xs, yh, tv, den_v, ext,
    ym_s, ym_r, ya_s, ya_r, xb_s, xb_r, xg_s, xg_r, hop_r, rlx, nu_s, nu_r,
    in_sem, pl_s, pl_r, ym_ss, ym_rs, ya_ss, ya_rs, xb_ss, xb_rs, xg_ss, xg_rs, hop_ss, hop_rs, on_ss, nu_ss, nu_rs,
    x_in, y_in, left_in, strong,
):
    gx, gy, core = lax.axis_index("gx"), lax.axis_index("gy"), lax.axis_index("depth")
    n_gx, n_gy = lax.axis_size("gx"), lax.axis_size("gy")
    has_x = (gx > 0, gx < n_gx - 1)
    has_y = (gy > 0, gy < n_gy - 1)
    to_x = ({"gx": gx - 1}, {"gx": gx + 1})
    to_y = ({"gy": gy - 1}, {"gy": gy + 1})
    to_p = {"depth": 1 - core}

    barrier = pltpu.get_barrier_semaphore()

    def tell(device):
        pl.semaphore_signal(barrier, inc=1, device_id=device, device_id_type=MESH)

    tell(to_p)
    for d in range(2):
        told = has_x[d] & (gx % 8 > 0 if d == 0 else gx % 8 < 7)
        pl.when(told)(functools.partial(tell, {**to_x[d], "depth": 0}))
        pl.when(has_y[d])(functools.partial(tell, {**to_y[d], "depth": 1}))

    def know(counter, other_sem, has):
        @pl.when(core == counter)
        def _():
            pl.semaphore_wait(barrier, 1 + 2 * sum(one.astype(jnp.int32) for one in has))
            pl.semaphore_signal(other_sem, inc=1, device_id=to_p, device_id_type=MESH)

        @pl.when(core != counter)
        def _():
            pl.semaphore_wait(other_sem, 1)

    early, late = has_x[0] & (gx % 8 == 0), has_x[1] & (gx % 8 == 7)

    def know_x():
        know(0, x_in, (has_x[0] & (gx % 8 > 0), has_x[1]))

        @pl.when(late)
        def _():
            pl.semaphore_signal(left_in, inc=1, device_id=to_x[1], device_id_type=MESH)


    def know_y():
        know(1, y_in, has_y)
        pl.when(early)(functools.partial(tell, {**to_x[0], "depth": 0}))

    loads = [
        pltpu.make_async_copy(mom, momv, in_sem.at[19]),
        pltpu.make_async_copy(des, desv, in_sem.at[20]),
        pltpu.make_async_copy(sol, solv, in_sem.at[21]),
        pltpu.make_async_copy(por, porv, in_sem.at[22]),
    ]
    for i in range(19):
        start = PAD + (16 if C[i][2] == -1 else 0)
        loads.append(pltpu.make_async_copy(adj.at[i], adjv.at[i, pl.ds(start, 192), :], in_sem.at[i]))
    for copy in loads:
        copy.start()

    for d in range(2):

        def clear_x(d=d):
            xb_r[d] = jnp.zeros_like(xb_r[d])

        def clear_y(d=d):
            for ref in (ym_r, ya_r):
                ref[d] = jnp.zeros_like(ref[d])

        pl.when(jnp.logical_not(has_x[d]))(clear_x)
        pl.when(jnp.logical_not(has_y[d]))(clear_y)
        for e in range(2):

            def clear_xy(d=d, e=e):
                xg_r[2 * d + e] = jnp.zeros_like(xg_r[2 * d + e])

            pl.when(jnp.logical_not(has_x[d] & has_y[e]))(clear_xy)

    @pl.when(core == 0)
    def _():
        for i in ZD:
            adjv[i, PAD : PAD + 16, :] = jnp.zeros((16, 128), F32)

    @pl.when(core == 1)
    def _():
        for i in ZU:
            adjv[i, PAD + 192 : PAD + 208, :] = jnp.zeros((16, 128), F32)

    def planes(pops, src_row):
        return [
            pltpu.make_async_remote_copy(
                src_ref=adj.at[i, pl.ds(src_row, 16), :],
                dst_ref=halo.at[j],
                send_sem=pl_s.at[j],
                recv_sem=pl_r.at[j],
                device_id=to_p,
                device_id_type=MESH,
            )
            for j, i in enumerate(pops)
        ]

    plane_down = planes(ZD, 176)
    plane_up = planes(ZU, 0)

    def send_planes():
        @pl.when(core == 0)
        def _():
            for copy in plane_down:
                copy.start()

        @pl.when(core == 1)
        def _():
            for copy in plane_up:
                copy.start()

    know_x()
    send_planes()

    def remote(src, dst, s_sem, r_sem, d, device):
        return pltpu.make_async_remote_copy(
            src_ref=src.at[d] if src is not xb_s else src.at[d, pl.ds(0, 28), :],
            dst_ref=dst.at[1 - d],
            send_sem=s_sem.at[d],
            recv_sem=r_sem.at[1 - d],
            device_id=device,
            device_id_type=MESH,
        )

    cxb = [remote(xb_s, xb_r, xb_ss, xb_rs, d, to_x[d]) for d in range(2)]
    cym = [remote(ym_s, ym_r, ym_ss, ym_rs, d, to_y[d]) for d in range(2)]
    cya = [remote(ya_s, ya_r, ya_ss, ya_rs, d, to_y[d]) for d in range(2)]
    cxg = [
        [
            pltpu.make_async_remote_copy(
                src_ref=xg_s.at[2 * d + e],
                dst_ref=xg_r.at[2 * (1 - d) + 1 - e],
                send_sem=xg_ss.at[2 * d + e],
                recv_sem=xg_rs.at[2 * (1 - d) + 1 - e],
                device_id={**to_x[d], **to_y[e]},
                device_id_type=MESH,
            )
            for e in range(2)
        ]
        for d in range(2)
    ]
    hop = [
        pltpu.make_async_remote_copy(
            src_ref=xg_s.at[e],
            dst_ref=hop_r.at[e],
            send_sem=hop_ss.at[e],
            recv_sem=hop_rs.at[e],
            device_id=to_x[0],
            device_id_type=MESH,
        )
        for e in range(2)
    ]
    onward = [
        pltpu.make_async_remote_copy(
            src_ref=hop_r.at[e],
            dst_ref=xg_r.at[3 - e],
            send_sem=on_ss.at[e],
            recv_sem=xg_rs.at[3 - e],
            device_id=to_y[e],
            device_id_type=MESH,
        )
        for e in range(2)
    ]
    cnu = pltpu.make_async_remote_copy(
        src_ref=nu_s, dst_ref=nu_r, send_sem=nu_ss.at[0], recv_sem=nu_rs.at[0], device_id=to_p, device_id_type=MESH
    )

    for copy in loads[:4]:
        copy.wait()

    slope3 = 3.0 / ((1.0 + desv[...]) * (1.0 + desv[...]))

    @pl.loop(0, 12)
    def _(z):
        rows = pl.ds(pl.multiple_of(z * 16, 16), 16)
        keep = (solv[rows, :] == 0) & (porv[rows, :] != 1)
        scale = jnp.where(keep, slope3, 0.0)
        for k in range(3):
            mv[k, rows, :] = scale * momv[k, rows, :]

    for copy in loads[4:]:
        copy.wait()

    zo = [PAD + (16 if C[i][2] == 1 else 0) for i in range(19)]
    lane12 = lane_of((12, 128))
    lane8 = lane_of((8, 128))

    def pack(d, z, cp, cm):
        edge = 127 if d == 1 else 0
        pops = XL if d == 1 else XR
        for h in range(2):
            row = pl.multiple_of(z * 16, 16) + 8 * h
            for j in range(5):
                here = lane8 == 2 * z + h + BLK * j
                v = adjv[pops[j], pl.ds(zo[pops[j]] + row, 8), :]
                cp = jnp.where(here, jnp.broadcast_to(v[:, edge : edge + 1], (8, 128)), cp)
                if j < 3:
                    m = mv[j, pl.ds(row, 8), :]
                    cm = jnp.where(here, jnp.broadcast_to(m[:, edge : edge + 1], (8, 128)), cm)
        return cp, cm

    lane16, row16 = lane_of((16, 128)), row_of((16, 128))

    def inner(z, total):
        base = pl.multiple_of(z * 16, 16)
        last, first = row16 == 15, row16 == 0

        def at(i):
            return adjv[i, pl.ds(zo[i] + base + C[i][1], 16), :]

        def up(v):
            return jnp.where(last, 0.0, v)

        def down(v):
            return jnp.where(first, 0.0, v)

        def right(v):
            return jnp.where(lane16 == 127, 0.0, roll(v, -1, 1))

        def left(v):
            return jnp.where(lane16 == 0, 0.0, roll(v, 1, 1))

        v7, v9, v8, v10 = up(at(7)), down(at(9)), down(at(8)), up(at(10))
        v11, v13, v12, v14 = at(11), at(13), at(12), at(14)
        x_sum = right((2.0 * at(1) + v7) + (v9 + v11) + v13) - left((2.0 * at(2) + v8) + (v10 + v12) + v14)
        v15, v17, v16, v18 = at(15), at(17), at(16), at(18)
        y_sum = up((2.0 * at(3) + v15) + v17) - down((2.0 * at(4) + v16) + v18)
        y_sum = y_sum + right(v7 - v9) + left(v10 - v8)
        z_sum = 2.0 * (at(5) - at(6)) + up(v15 - v17) + down(v18 - v16)
        z_sum = z_sum + right(v11 - v13) + left(v14 - v12)
        return (
            total
            + x_sum * mv[0, pl.ds(base, 16), :]
            + y_sum * mv[1, pl.ds(base, 16), :]
            + z_sum * mv[2, pl.ds(base, 16), :]
        )

    def both(z, carry):
        return (*pack(1, z, *carry[:2]), inner(z, carry[2]))

    zero8 = jnp.zeros((8, 128), F32)
    carry = lax.fori_loop(
        0, 11, lambda k, c: both(k + core, c), (zero8, zero8, jnp.zeros((16, 128), F32)), unroll=True
    )

    @pl.when(core == 0)
    def _():
        for copy in plane_up:
            copy.wait_recv()
        for j, i in enumerate(ZU):
            adjv[i, PAD + 192 : PAD + 208, :] = halo[j]

    @pl.when(core == 1)
    def _():
        for copy in plane_down:
            copy.wait_recv()
        for j, i in enumerate(ZD):
            adjv[i, PAD : PAD + 16, :] = halo[j]

    cp1, cm1, a0 = both(11 * (1 - core), carry)
    a0 = a0 * (1.0 / 36.0)

    def with_strips(d, cm):
        for h in range(2):
            first = STRIP + 4 * h
            moved = roll(a0[8 * h : 8 * h + 8], first - (124 if d == 1 else 0), 1)
            cm = jnp.where((lane8 >= first) & (lane8 < first + 4), moved, cm)
        return cm

    xb_s[1, 0:8, :] = cp1
    xb_s[1, 8:16, :] = with_strips(1, cm1)

    edge_rows = []
    for d, (pops, row) in enumerate(((YU, 0), (YD, 15))):
        values = [adjv[i, pl.ds(zo[i] + row, 12, stride=16), :] for i in pops]
        values += [mv[k, pl.ds(row, 12, stride=16), :] for k in range(3)]
        edge_rows.append(values)
        for v in range(8):
            ym_s[d, v] = values[v]
    def pack_rows(d):
        packed = jnp.zeros((12, 128), F32)
        for l in range(2):
            for v in range(8):
                slot = 64 * l + 8 * v
                moved = roll(edge_rows[l][v], slot - (0 if d == 0 else 120), 1)
                packed = jnp.where((lane12 >= slot) & (lane12 < slot + 8), moved, packed)
        xb_s[d, 16:28, :] = packed

    def pack_corners(d):
        head, tail = xb_s[d, 16:24, :], xb_s[d, 24:32, :]
        for e in range(2):
            xg_s[2 * d + e, 0:8, :] = joined(xb_s[d, 0:8, :], xb_s[d, 8:16, :], e)
            if e == 0:
                xg_s[2 * d + e, 8:16, :] = jnp.where(lane8 < 64, head, roll(tail, 64, 1))
            else:
                xg_s[2 * d + e, 8:16, :] = jnp.where(lane8 < 64, roll(head, 64, 1), tail)

    def send_x(d):
        pl.when(has_x[d])(cxb[d].start)

    def send_xy(d, when):
        for e in range(2):
            pl.when(when & has_x[d] & has_y[e])(cxg[d][e].start)

    def send_y():
        for d in range(2):
            ya_s[d, 0:8, :] = a0[8 * d : 8 * d + 8]
            ya_s[d, 8:16, :] = xg_s[d, 0:8, :]
            ya_s[d, 16:24, :] = xg_s[2 + d, 0:8, :]
            pl.when(has_y[d])(cym[d].start)
            pl.when(has_y[d])(cya[d].start)

    def tell_strong():
        for d in range(2):
            pl.when(has_x[d] & (gx % 8 > 0 if d == 0 else gx % 8 < 7))(
                functools.partial(pl.semaphore_signal, strong.at[1 - d], inc=1, device_id=to_x[d], device_id_type=MESH)
            )

    for d in range(2):
        xb_s[d, 24:32, :] = zero8
    pack_rows(1)
    pack_corners(1)

    send_x(1)
    send_xy(1, late)

    cp0, cm0 = lax.fori_loop(0, 12, lambda z, carry: pack(0, z, *carry), (zero8, zero8))
    xb_s[0, 0:8, :] = cp0
    xb_s[0, 8:16, :] = with_strips(0, cm0)
    pack_rows(0)
    pack_corners(0)

    pl.when(jnp.logical_not(early))(functools.partial(send_x, 0))
    know_y()
    send_y()
    tell_strong()

    def send_left():
        pl.semaphore_wait(strong.at[0], 1)
        send_xy(0, True)

    def send_right():
        pl.semaphore_wait(strong.at[1], 1)
        send_xy(1, True)

    pl.when(has_x[0] & (gx % 8 > 1))(send_left)
    pl.when(has_x[1] & (gx % 8 < 7))(send_right)
    pl.when(has_x[0] & (gx % 8 == 1))(send_left)

    for e in range(2):

        @pl.when(late & has_y[e])
        def _(e=e):
            hop[e].wait_recv()
            onward[e].start()

    @pl.when(early)
    def _():
        pl.semaphore_wait(left_in, 1)
        send_x(0)
        for e in range(2):
            pl.when(has_y[e])(hop[e].start)

    row8 = row_of((8, 128))
    ones, ones_out = [], []
    for k in range(4):
        y = gy * 16 + (row8 + (8 * k - 8))
        inside = (y >= 0) & (y < 16 * n_gy)
        ones.append(jnp.where(inside, 1.0, 0.0))
        x_out = jnp.where(lane8 < 64, gx * 128 + 128 + lane8, gx * 128 - 128 + lane8)
        ones_out.append(jnp.where(inside & (x_out >= 0) & (x_out < 128 * n_gx), 1.0, 0.0))
    den_v[...] = filtered(ones, ones_out, tv)

    for d in range(2):
        pl.when(has_x[d])(cxb[1 - d].wait_recv)
    cp_l, cm_l, left = xb_r[0, 0:8, :], xb_r[0, 8:16, :], xb_r[0, 16:28, :]
    cp_r, cm_r, right = xb_r[1, 0:8, :], xb_r[1, 8:16, :], xb_r[1, 16:28, :]

    def with_x_terms(inside, near, far, ends_of, halves):
        (np0, nm0, np1, nm1), (fp0, fm0, fp1, fm1) = near, far
        own = (x_terms(XL, nm0, fp0, halves), x_terms(XR, nm1, fp1, halves))
        theirs = (x_terms(XR, fm0, np0, halves), x_terms(XL, fm1, np1, halves))
        out = []
        for n, h in enumerate(halves):
            main = inside[n] + jnp.where(lane8 == 0, own[0][n], 0.0) + jnp.where(lane8 == 127, own[1][n], 0.0)
            outer = ends_of[n]
            outer = outer + jnp.where(lane8 == 127, theirs[0][n], 0.0) + jnp.where(lane8 == 0, theirs[1][n], 0.0)
            out.append([main, outer])
        return out

    blocks = with_x_terms([a0[0:8], a0[8:16]], (cp0, cm0, cp1, cm1), (cp_l, cm_l, cp_r, cm_r), [strips(cm_l, cm_r, STRIP + 4 * h) for h in range(2)], (0, 1))

    def move(z, carry):
        for h in range(2):
            row = pl.multiple_of(z * 16, 16) + 8 * h
            for n, i in enumerate(XS):
                at = 2 * z + h + BLK * (n % 5)
                v = adjv[i, pl.ds(zo[i] + row, 8), :]
                if n < 5:
                    v = jnp.where(lane8 == 127, roll(cp_r, 127 - at, 1), roll(v, -1, 1))
                else:
                    v = jnp.where(lane8 == 0, roll(cp_l, 128 - at, 1), roll(v, 1, 1))
                xs[n, pl.ds(PAD + row, 8), :] = v
        return carry

    lax.fori_loop(0, 12, move, 0)

    def ends(from_right, from_left, at_right, at_left):
        a = roll(from_right, -at_right, 1)
        b = roll(from_left, 120 - at_left, 1)
        return jnp.where(lane12 < 8, a, jnp.where(lane12 >= 120, b, 0.0))

    own_outer = [[ends(right, left, 64 * l + 8 * v, 64 * l + 8 * v) for v in range(8)] for l in range(2)]

    for d in range(2):
        pl.when(has_y[d])(cym[1 - d].wait_recv)
        pl.when(has_y[d])(cya[1 - d].wait_recv)
    for d in range(2):
        for e in range(2):
            pl.when(has_x[d] & has_y[e])(cxg[1 - d][1 - e].wait_recv)

    def weighted(pops, moms, pulled):
        total = None
        for j, i in enumerate(pops):
            c = C[i]
            u = None
            for k in range(3):
                if c[k] != 0:
                    u = (moms[k] if c[k] == 1 else -moms[k]) if u is None else (u + moms[k] if c[k] == 1 else u - moms[k])
            term = (W[i] * u) * pulled[j]
            total = term if total is None else total + term
        return jnp.sum(total, axis=0, keepdims=True)

    for n in range(4):
        rlx[n, 0:8, :] = xg_r[n, 8:16, :]
        rlx[n, 8:16, :] = roll(xg_r[n, 8:16, :], 64, 1)
    inside_rows, beyond_rows = [], []
    for d, (mine, others) in enumerate(((YU, YD), (YD, YU))):
        got = [ym_r[d, v] for v in range(8)]
        far_left, far_right = rlx[d, 0:12, :], rlx[2 + d, 0:12, :]
        got_outer = [ends(far_right, far_left, 8 * v, 8 * v) for v in range(8)]
        moved = [shift_ext(got[j], got_outer[j], C[others[j]][0]) for j in range(5)]
        for j in range(5):
            yh[d, j] = moved[j][0]
        inside_rows.append(
            (
                weighted(others, edge_rows[d][5:], [m[0] for m in moved]),
                weighted(others, own_outer[d][5:], [m[1] for m in moved]),
            )
        )
        moved = [shift_ext(edge_rows[d][j], own_outer[d][j], C[mine[j]][0]) for j in range(5)]
        beyond_rows.append(
            (weighted(mine, got[5:], [m[0] for m in moved]), weighted(mine, got_outer[5:], [m[1] for m in moved]))
        )

    beyond = []
    for e in range(2):
        near = (*parted(ya_r[e, 8:16, :]), *parted(ya_r[e, 16:24, :]))
        got_l, got_r = xg_r[e, 0:8, :], xg_r[2 + e, 0:8, :]
        far = (*parted(got_l), *parted(got_r))
        beyond += with_x_terms([ya_r[e, 0:8, :]], near, far, [strips(got_l, got_r, 120)], (0,))
    blocks = [beyond[0], *blocks, beyond[1]]
    for part in range(2):
        blocks[0][part] = blocks[0][part] + jnp.where(row8 == 7, beyond_rows[0][part], 0.0)
        blocks[1][part] = blocks[1][part] + jnp.where(row8 == 0, inside_rows[0][part], 0.0)
        blocks[2][part] = blocks[2][part] + jnp.where(row8 == 7, inside_rows[1][part], 0.0)
        blocks[3][part] = blocks[3][part] + jnp.where(row8 == 0, beyond_rows[1][part], 0.0)
    number = filtered([b[0] for b in blocks], [b[1] for b in blocks], tv)
    nu_s[...] = number
    cnu.start()

    damping = 0.5 * (1.0 - desv[...]) / (1.0 + desv[...])

    @pl.loop(0, 12)
    def _(z):
        base = pl.multiple_of(z * 16, 16)
        rows = pl.ds(base, 16)
        pulled = []
        for i in range(19):
            c = C[i]
            if c[0] != 0:
                v = xs[XS.index(i), pl.ds(PAD + base + c[1], 16), :]
            else:
                v = adjv[i, pl.ds(zo[i] + base + c[1], 16), :]
            if c[1] == 1:
                v = jnp.where(row16 == 15, yh[1, YU.index(i), pl.ds(z, 1), :], v)
            elif c[1] == -1:
                v = jnp.where(row16 == 0, yh[0, YD.index(i), pl.ds(z, 1), :], v)
            pulled.append(v)
        zeroth = W[0] * pulled[0]
        sums = [jnp.zeros((16, 128), F32)] * 3
        for i in range(1, 19):
            v = W[i] * pulled[i]
            zeroth = zeroth + v
            for k in range(3):
                if C[i][k] == 1:
                    sums[k] = sums[k] + v
                elif C[i][k] == -1:
                    sums[k] = sums[k] - v
        gain = (1.25 - damping) * 3.0
        sums = [gain * s for s in sums]
        base_term = 1.25 * zeroth
        fluid = solv[rows, :] == 0
        port = porv[rows, :]
        inlet, outlet = port == 1, port == 2
        bump = jnp.where(outlet, 1.0, 0.0)
        for i in range(19):
            c = C[i]
            relaxed = base_term - 0.25 * pulled[i]
            for k in range(3):
                if c[k] == 1:
                    relaxed = relaxed + sums[k]
                elif c[k] == -1:
                    relaxed = relaxed - sums[k]
            out = jnp.where(fluid, relaxed, pulled[OPP[i]])
            out = jnp.where(inlet, 0.0, out)
            if c[0] == 1:
                out = out + bump
            elif c[0] == -1:
                out = out - bump
            new[i, rows, :] = out

    cnu.wait_recv()
    sens[...] = (number + nu_r[...]) / den_v[...]

    @pl.when(core == 0)
    def _():
        for copy in plane_down:
            copy.wait_send()

    @pl.when(core == 1)
    def _():
        for copy in plane_up:
            copy.wait_send()

    for d in range(2):
        pl.when(has_x[d])(cxb[d].wait_send)
        for copy in (cym[d], cya[d]):
            pl.when(has_y[d])(copy.wait_send)
        for e in range(2):
            direct = has_x[d] & has_y[e] & (gx % 8 > 0) if d == 0 else has_x[d] & has_y[e]
            pl.when(direct)(cxg[d][e].wait_send)
        pl.when(early & has_y[d])(hop[d].wait_send)
        pl.when(late & has_y[d])(onward[d].wait_send)
    cnu.wait_send()


def write_out(new_v, sens_v, new, sens, sem):
    copies = [pltpu.make_async_copy(new_v.at[i], new.at[i], sem.at[i]) for i in range(19)]
    copies.append(pltpu.make_async_copy(sens_v, sens, sem.at[19]))
    for copy in copies:
        copy.start()
    for copy in copies:
        copy.wait()


def on_device(adjoint, momentum, design, solid_mask, port_label):
    hbm = pl.BlockSpec(memory_space=pl.ANY)
    vmem = pl.BlockSpec(memory_space=pltpu.VMEM)
    dma = pltpu.SemaphoreType.DMA
    v = lambda *shape, t=F32: pltpu.VMEM(shape, t)
    buffers = [
        v(19, 224, 128), v(5, 16, 128), v(3, 192, 128), v(16, 128), v(192, 128, t=jnp.int32), v(192, 128, t=jnp.int32),
        v(3, 192, 128), v(10, 208, 128), v(2, 5, 12, 128), v(5, 32, 128), v(16, 128), v(8, 128),
    ]
    buffers += [v(2, 8, 12, 128), v(2, 8, 12, 128), v(2, 24, 128), v(2, 24, 128), v(2, 32, 128), v(2, 28, 128)]
    buffers += [v(4, 16, 128), v(4, 16, 128), v(2, 16, 128), v(4, 16, 128)]
    buffers += [v(16, 128), v(16, 128)]
    regular = pltpu.SemaphoreType.REGULAR
    sems = [dma((23,)), dma((5,)), dma((5,))] + [dma((2,))] * 6 + [dma((4,))] * 2 + [dma((2,))] * 3 + [dma((1,))] * 2
    sems += [regular, regular, regular, regular((2,))]
    new, sens = pl.pallas_call(
        kernel,
        out_shape=(v(19, 192, 128), v(16, 128)),
        in_specs=[hbm] * 5,
        out_specs=(vmem, vmem),
        scratch_shapes=buffers + sems,
        compiler_params=pltpu.CompilerParams(collective_id=0, has_side_effects=True),
    )(
        adjoint.reshape(19, 192, 128),
        momentum.reshape(3, 192, 128),
        design,
        solid_mask.reshape(192, 128),
        port_label.reshape(192, 128),
    )
    new, sens = pl.pallas_call(
        write_out,
        out_shape=(jax.ShapeDtypeStruct((19, 192, 128), F32), jax.ShapeDtypeStruct((16, 128), F32)),
        in_specs=[vmem, vmem],
        out_specs=(hbm, hbm),
        scratch_shapes=[dma((20,))],
    )(*(pltpu.with_memory_space_constraint(x, pltpu.VMEM) for x in (new, sens)))
    return new.reshape(19, 12, 16, 128), sens


def solution(mesh):
    cells = P("depth", "gy", "gx")
    fields = P(None, "depth", "gy", "gx")
    plane = P("gy", "gx")
    return jax.shard_map(
        on_device,
        mesh=mesh,
        in_specs=(fields, fields, plane, cells, cells),
        out_specs=(fields, plane),
        check_vma=False,
    )
```
